512 devices in a mesh: ctx: 32 (over z, core), bal: 16 (over x, y).
Axes of the slice: x: 4, y: 4, z: 16, core: 2. Of those that a mesh axis runs over, the one named last changes fastest.
Arguments:
- xbc: bfloat16 [16, 8192, 2688], P('bal', 'ctx'), may hold values from -6 to 6
- dt_raw: bfloat16 [16, 8192, 40], P('bal', 'ctx'), may hold values from -4 to 4
- conv_weight: float32 [4, 2688], replicated, may hold values from -3 to 3
- conv_bias: float32 [2688], replicated, may hold values from -0.5 to 0.5
- dt_bias: float32 [40], replicated, may hold values from -3 to 0
- a_log: float32 [40], replicated, may hold values from -9.2 to -2.3
- d_skip: float32 [40], replicated, may hold values from 0.5 to 1.5
- grad_out: bfloat16 [16, 8192, 2560], P('bal', 'ctx'), may hold values from -6 to 6
- doc_lengths: int32 [16, 8], P('bal'), may hold values from 1 to 4096, 8192 in all within a row
Outputs:
- grad_xbc: bfloat16 [16, 8192, 2688], P('bal', 'ctx')
- grad_dt_raw: bfloat16 [16, 8192, 40], P('bal', 'ctx')
- grad_conv_weight: float32 [4, 2688], replicated
- grad_conv_bias: float32 [2688], replicated
- grad_dt_bias: float32 [40], replicated
- grad_a_log: float32 [40], replicated
- grad_d_skip: float32 [40], replicated
The draws below stay inside these ranges and needn't reach their ends.
Inputs may be any that keep to these rules, and one draw needn't show every extreme that they name: `doc_lengths`: each row sums to 8192; its largest entry is exactly 4096.
All inputs are finite; a program needn't handle non-finite values.
Results may differ from the reference program's by a relative error of at most 0.013.
Values may be sent and summed in bfloat16 or wider, within the bound.
A program may use at most 128 MiB of HBM per device.

```python
import math
import jax
import jax.numpy as jnp
import numpy as np
from jax import lax

H = 40
P_SIZE = 64
N = 64
G = 1
KW = 4
DOCS = 8
TOK = 256
DIN = 2560
CH = 2688
SEQ = 8192
GROUPS = 16
MOST = 4096
N_CTX = 32


def block_levels(own_key, shape, split, low, largest):
    loudness = 1.0
    for dim, blocks in split:
        draws = jax.random.uniform(jax.random.fold_in(jax.random.fold_in(own_key, 6), dim), (blocks,), jnp.float32, low / len(split), largest / len(split))
        loudness = loudness * jnp.repeat(jnp.exp(draws), shape[dim] // blocks).reshape((-1,) + (1,) * (len(shape) - 1 - dim))
    return loudness


def profile(count, total, most, lean):
    weights = [(1 << 20) // math.isqrt(rank ** lean) + 1 for rank in range(2, count + 1)]
    spare, holding = total - most - (count - 1), [1] * (count - 1)
    while spare > 0:
        movable = [i for i in range(count - 1) if holding[i] < most]
        mass, budget = sum([weights[i] for i in movable]), spare
        for i in movable:
            more = min(most - holding[i], max(1, budget * weights[i] // mass), spare)
            holding[i] = holding[i] + more
            spare = spare - more
    return np.array([most] + holding)


def ragged(key, amount, total, reach, skew):
    if amount == 2:
        one = jax.random.randint(key, (), max(1, total - reach), min(reach, total - 1) + 1)
        return jnp.stack([one, total - one])
    sizes = jnp.asarray(profile(amount, total, reach, skew), jnp.int32)
    couples = (amount - 1) // 2
    donor, receiver = sizes[1:1 + 2 * couples:2], sizes[2:2 + 2 * couples:2]
    margin = jnp.minimum(donor - 1, reach - receiver)
    passed = jax.random.randint(jax.random.fold_in(key, 1), (couples,), 0, 1 << 20) % (margin + 1)
    sizes = sizes.at[1:1 + 2 * couples:2].set(donor - passed).at[2:2 + 2 * couples:2].set(receiver + passed)
    return sizes[jax.random.permutation(jax.random.fold_in(key, 2), amount)]


def scatter_about(stream_key, dims, width, limit, shards=(), kind=jnp.bfloat16):
    result = width * jax.random.normal(stream_key, dims, jnp.float32)
    if shards:
        result = result * block_levels(stream_key, dims, shards, -0.22, 0.18)
    return jnp.clip(result, -limit, limit).astype(kind)


def setup_inputs(seed: int = 0) -> dict:
    key_of = jax.random.split(jax.random.key(seed), 10)
    return {
        "xbc": scatter_about(key_of[0], (GROUPS, SEQ, CH), 1.0, 6.0, ((0, 16), (1, 32))),
        "dt_raw": scatter_about(key_of[1], (GROUPS, SEQ, H), 1.0, 4.0, ((0, 16), (1, 32))),
        "conv_weight": scatter_about(key_of[2], (KW, CH), 0.5, 3.0, (), jnp.float32),
        "conv_bias": jnp.clip(jax.random.uniform(key_of[3], (CH,), jnp.float32, -0.5, 0.5), -0.5, 0.5),
        "dt_bias": jnp.clip(jax.random.uniform(key_of[4], (H,), jnp.float32, -3.0, 0.0), -3.0, 0.0),
        "a_log": jnp.clip(jax.random.uniform(key_of[5], (H,), jnp.float32, -9.2, -2.3), -9.2, -2.3),
        "d_skip": jnp.clip(jax.random.uniform(key_of[6], (H,), jnp.float32, 0.5, 1.5), 0.5, 1.5),
        "grad_out": scatter_about(key_of[7], (GROUPS, SEQ, DIN), 1.0, 6.0, ((0, 16), (1, 32))),
        "doc_lengths": jax.vmap(lambda own: ragged(own, DOCS, SEQ, MOST, 2))(jax.random.split(key_of[8], GROUPS)).reshape((GROUPS, DOCS)).astype(jnp.int32),
    }


HIGHEST = lax.Precision.HIGHEST

def doc_index(lengths, positions):
    lengths = lengths.astype(jnp.int32)
    starts = (jnp.cumsum(lengths) - lengths).astype(jnp.int32)
    hits = (positions[:, None] >= starts[None, :]).astype(jnp.int32)
    return (lax.optimization_barrier(jnp.sum(hits, axis=1)) - 1).astype(jnp.int32)

def split_act(activated):
    length = activated.shape[0]
    xpart = activated[:, :H * P_SIZE].reshape(length, H, P_SIZE)
    bpart = activated[:, H * P_SIZE:H * P_SIZE + G * N].reshape(length, G, N)
    cpart = activated[:, H * P_SIZE + G * N:].reshape(length, G, N)
    return (xpart, bpart, cpart)

def prepare(extended, raw_steps, conv_weight, conv_bias, dt_bias, a_log, docs_ext):
    kernel_len = conv_weight.shape[0]
    length = raw_steps.shape[0]
    own_docs = docs_ext[kernel_len - 1:]
    wide = extended.astype(jnp.float32)
    pre = jnp.zeros((length, wide.shape[1]), jnp.float32) + conv_bias[None, :]
    for lag_index in range(kernel_len):
        keep = (docs_ext[lag_index:lag_index + length] == own_docs).astype(jnp.float32)
        pre = pre + conv_weight[lag_index][None, :] * wide[lag_index:lag_index + length] * keep[:, None]
    activated = jax.nn.silu(pre).astype(jnp.bfloat16)
    xpart, bpart, cpart = split_act(activated)
    step_size = jax.nn.softplus(raw_steps.astype(jnp.float32) + dt_bias[None, :])
    cumulative = jnp.cumsum(step_size * (-jnp.exp(a_log))[None, :], axis=0)
    same_last = (own_docs == own_docs[-1]).astype(jnp.float32)
    tail = jnp.exp(cumulative[-1][None, :] - cumulative) * same_last[:, None] * step_size
    weighted = (xpart.astype(jnp.float32) * tail[:, :, None]).astype(jnp.bfloat16)
    weighted = weighted.reshape(length, G, H // G, P_SIZE)
    local_state = jnp.einsum('sgkp,sgn->gkpn', weighted, bpart, preferred_element_type=jnp.float32).reshape(H, P_SIZE, N)
    carried = (own_docs[-1] == docs_ext[kernel_len - 2]).astype(jnp.float32)
    total_decay = jnp.exp(cumulative[-1]) * carried
    return (activated, step_size, cumulative, local_state, total_decay)

def mixing(activated, step_size, cumulative, d_skip, incoming, own_docs, prev_doc):
    length = activated.shape[0]
    xpart, bpart, cpart = split_act(activated)
    scores = jnp.einsum('tgn,sgn->gts', cpart, bpart, preferred_element_type=jnp.float32)
    scores = jnp.repeat(scores, H // G, axis=0)
    order = jnp.arange(length, dtype=jnp.int32)
    same = (own_docs[:, None] == own_docs[None, :]) & (order[:, None] >= order[None, :])
    gap = cumulative.T[:, :, None] - cumulative.T[:, None, :]
    decay = jnp.where(same[None], jnp.exp(jnp.minimum(gap, 0.0)), 0.0)
    weights = (scores * decay * step_size.T[:, None, :]).astype(jnp.bfloat16)
    inner = jnp.einsum('hts,shp->thp', weights, xpart, preferred_element_type=jnp.float32)
    lead = jnp.exp(cumulative) * (own_docs == prev_doc).astype(jnp.float32)[:, None]
    outer = jnp.einsum('tgn,gkpn->tgkp', cpart.astype(jnp.float32), incoming.reshape(G, H // G, P_SIZE, N), precision=HIGHEST)
    outer = outer.reshape(length, H, P_SIZE)
    return inner + lead[:, :, None] * outer + d_skip[None, :, None] * xpart.astype(jnp.float32)

def seed_state(activated, cumulative, cot_out, own_docs, prev_doc):
    length = activated.shape[0]
    xpart, bpart, cpart = split_act(activated)
    lead = jnp.exp(cumulative) * (own_docs == prev_doc).astype(jnp.float32)[:, None]
    scaled = (lead[:, :, None] * cot_out).reshape(length, G, H // G, P_SIZE)
    seeded = jnp.einsum('tgn,tgkp->gkpn', cpart.astype(jnp.float32), scaled, precision=HIGHEST)
    return seeded.reshape(H, P_SIZE, N)

def reference(xbc, dt_raw, conv_weight, conv_bias, dt_bias, a_log, d_skip, grad_out, doc_lengths):
    kernel_len = conv_weight.shape[0]
    length = TOK
    padded = jnp.pad(xbc, ((0, 0), (kernel_len - 1, 0), (0, 0)))
    positions = jnp.arange(SEQ + kernel_len - 1, dtype=jnp.int32) - (kernel_len - 1)
    docs_all = jax.vmap(lambda lens: doc_index(lens, positions))(doc_lengths)

    def slice_inputs(block):
        start = (block * length).astype(jnp.int32)
        extended = lax.dynamic_slice_in_dim(padded, start, length + kernel_len - 1, 1)
        raw_steps = lax.dynamic_slice_in_dim(dt_raw, start, length, 1)
        cot_rows = lax.dynamic_slice_in_dim(grad_out, start, length, 1)
        docs_ext = lax.dynamic_slice_in_dim(docs_all, start, length + kernel_len - 1, 1)
        return (extended, raw_steps, cot_rows, docs_ext)

    def prep_one(extended, raw_steps, docs_ext):
        return prepare(extended, raw_steps, conv_weight, conv_bias, dt_bias, a_log, docs_ext)

    def forward(state, block):
        extended, raw_steps, cot_rows, docs_ext = slice_inputs(block)
        prepared = jax.vmap(prep_one)(extended, raw_steps, docs_ext)
        local_state, total_decay = (prepared[3], prepared[4])
        return (total_decay[:, :, None, None] * state + local_state, state)
    start_state = jnp.zeros((GROUPS, H, P_SIZE, N), jnp.float32)
    blocks = jnp.arange(N_CTX, dtype=jnp.int32)
    _, states = lax.scan(forward, start_state, blocks)

    def slice_grads(extended, raw_steps, cot_rows, docs_ext, incoming, adjoint):

        def prep_fn(ext_in, raw_in, weight_in, bias_in, dtb_in, alog_in):
            return prepare(ext_in, raw_in, weight_in, bias_in, dtb_in, alog_in, docs_ext)
        prepared, pull_prep = jax.vjp(prep_fn, extended, raw_steps, conv_weight, conv_bias, dt_bias, a_log)
        activated, step_size, cumulative, local_state, total_decay = prepared
        own_docs = docs_ext[kernel_len - 1:]
        prev_doc = docs_ext[kernel_len - 2]

        def core_fn(act_in, step_in, cum_in, skip_in):
            return mixing(act_in, step_in, cum_in, skip_in, incoming, own_docs, prev_doc)
        _, pull_core = jax.vjp(core_fn, activated, step_size, cumulative, d_skip)
        cot_out = cot_rows.astype(jnp.float32).reshape(length, H, P_SIZE)
        grad_act, grad_step, grad_cum, grad_skip = pull_core(cot_out)
        seeded = seed_state(activated, cumulative, cot_out, own_docs, prev_doc)
        grad_total = lax.optimization_barrier(jnp.sum(adjoint * incoming, axis=(1, 2)))
        grad_ext, grad_raw, grad_weight, grad_bias, grad_dtb, grad_alog = pull_prep((grad_act, grad_step, grad_cum, adjoint, grad_total))
        return (grad_ext, grad_raw, (grad_weight, grad_bias, grad_dtb, grad_alog, grad_skip), seeded, total_decay)

    def backward(carry, block):
        adjoint, rim_back, sums = carry
        extended, raw_steps, cot_rows, docs_ext = slice_inputs(block)
        incoming = lax.dynamic_index_in_dim(states, block, 0, keepdims=False)
        grad_ext, grad_raw, param_grads, seeded, total_decay = jax.vmap(slice_grads)(extended, raw_steps, cot_rows, docs_ext, incoming, adjoint)
        new_adjoint = seeded + total_decay[:, :, None, None] * adjoint
        own_grad = grad_ext[:, kernel_len - 1:].astype(jnp.float32)
        own_grad = own_grad.at[:, length - kernel_len + 1:].add(rim_back.astype(jnp.float32))
        new_sums = tuple((total + lax.optimization_barrier(jnp.sum(part, axis=0)) for total, part in zip(sums, param_grads)))
        return ((new_adjoint, grad_ext[:, :kernel_len - 1], new_sums), (own_grad.astype(jnp.bfloat16), grad_raw))
    init_sums = (jnp.zeros((kernel_len, CH), jnp.float32), jnp.zeros((CH,), jnp.float32), jnp.zeros((H,), jnp.float32), jnp.zeros((H,), jnp.float32), jnp.zeros((H,), jnp.float32))
    init = (jnp.zeros((GROUPS, H, P_SIZE, N), jnp.float32), jnp.zeros((GROUPS, kernel_len - 1, CH), jnp.bfloat16), init_sums)
    reversed_blocks = jnp.arange(N_CTX - 1, -1, -1, dtype=jnp.int32)
    final, stacked = lax.scan(backward, init, reversed_blocks)
    grad_rows = jnp.flip(stacked[0], axis=0).transpose(1, 0, 2, 3).reshape(GROUPS, SEQ, CH)
    grad_steps = jnp.flip(stacked[1], axis=0).transpose(1, 0, 2, 3).reshape(GROUPS, SEQ, H)
    sums = final[2]
    return (grad_rows, grad_steps, sums[0], sums[1], sums[2], sums[3], sums[4])
```

```python
import jax
import jax.numpy as jnp
import numpy as np
from jax import lax
from jax.experimental import pallas as pl
from jax.experimental.pallas import tpu as pltpu
from jax.sharding import PartitionSpec as P

H = 40
P_SIZE = 64
N = 64
DIN = H * P_SIZE
PAIRS = H // 2
HIGHEST = lax.Precision.HIGHEST
F32 = jnp.float32
BF16 = jnp.bfloat16


def from_behind(value, axis, steps):
    count = lax.axis_size(axis)
    leading, last = (max(0, -steps), min(count, count - steps))
    return lax.ppermute(value, axis, [(source, source + steps) for source in range(leading, last)])


def doc_index(lengths, positions):
    starts = jnp.cumsum(lengths) - lengths
    hits = (positions[:, None] >= starts[None, :]).astype(jnp.int32)
    return jnp.sum(hits, axis=1) - 1


def dot(a, b, ca, cb, precision=None):
    return lax.dot_general(
        a, b, (((ca,), (cb,)), ((), ())), precision=precision, preferred_element_type=F32
    )


def core_kernel(
    x_ref, dy_ref, bc_ref, cumc_ref, cumr_ref, stepc_ref, docc_ref, docr_ref, skip_ref,
    dx_ref, xdx_ref, col_ref, xdy_ref, dbc_ref,
    scores, masked, gacc,
):
    j = pl.program_id(0)
    length = x_ref.shape[0]

    @pl.when(j == 0)
    def _():
        b, c = bc_ref[:, :N], bc_ref[:, N:]
        scores[...] = dot(b, c, 1, 1)
        s = lax.broadcasted_iota(jnp.int32, (length, length), 0)
        t = lax.broadcasted_iota(jnp.int32, (length, length), 1)
        same = (docc_ref[...] == docr_ref[...]) & (t >= s)
        masked[...] = jnp.where(same, 0.0, -1e30)
        gacc[...] = jnp.zeros_like(gacc)

    x, dy = x_ref[...], dy_ref[...]
    lane = lax.broadcasted_iota(jnp.int32, (length, 2 * P_SIZE), 1)
    mixes = []
    total = None
    for h in range(2):
        xh = jnp.where((lane < P_SIZE) == (h == 0), x, jnp.zeros_like(x))
        dw = dot(xh, dy, 1, 1)
        gap = cumr_ref[0, h : h + 1, :] - cumc_ref[0, :, h : h + 1]
        ds = jnp.exp(jnp.minimum(gap, 0.0) + masked[...]) * stepc_ref[0, :, h : h + 1]
        w = ds * scores[...]
        part = dw * ds
        total = part if total is None else total + part
        col_ref[0, h : h + 1, :] = jnp.sum(dw * w, axis=0, keepdims=True)
        mixes.append(dot(w.astype(BF16), dy, 1, 0))
    gacc[...] += total
    mix = jnp.where(lane < P_SIZE, mixes[0], mixes[1])
    xf, dyf = x.astype(F32), dy.astype(F32)
    xm = xf * mix
    first = jnp.sum(jnp.where(lane < P_SIZE, xm, 0.0), axis=1, keepdims=True)
    second = jnp.sum(jnp.where(lane < P_SIZE, 0.0, xm), axis=1, keepdims=True)
    xdx_ref[0] = jnp.concatenate([first, second], axis=1)
    xdy_ref[0] = jnp.sum(xf * dyf, axis=0, keepdims=True)
    dx_ref[...] = (mix + skip_ref[0] * dyf).astype(BF16)

    @pl.when(j == PAIRS - 1)
    def _():
        b, c = bc_ref[:, :N], bc_ref[:, N:]
        g = gacc[...].astype(BF16)
        dbc_ref[:, :N] = dot(g, c, 1, 0)
        dbc_ref[:, N:] = dot(g, b, 0, 0)


def core(activated, dy, cum, step, docs, skip_wide):
    length = activated.shape[0]
    pair_col = lambda v: v.reshape(length, PAIRS, 2).transpose(1, 0, 2)
    cumr = cum.T.reshape(PAIRS, 2, length)
    wide = pl.BlockSpec((length, 2 * P_SIZE), lambda j: (0, j))
    colspec = pl.BlockSpec((1, length, 2), lambda j: (j, 0, 0))
    rowspec = pl.BlockSpec((1, 2, length), lambda j: (j, 0, 0))
    lanes = pl.BlockSpec((1, 1, 2 * P_SIZE), lambda j: (j, 0, 0))
    dx, xdx, col, xdy, dbc = pl.pallas_call(
        core_kernel,
        grid=(PAIRS,),
        in_specs=[
            wide,
            wide,
            pl.BlockSpec((length, 2 * N), lambda j: (0, PAIRS)),
            colspec,
            rowspec,
            colspec,
            pl.BlockSpec((length, 1), lambda j: (0, 0)),
            pl.BlockSpec((1, length), lambda j: (0, 0)),
            lanes,
        ],
        out_specs=[
            wide,
            colspec,
            rowspec,
            lanes,
            pl.BlockSpec((length, 2 * N), lambda j: (0, 0)),
        ],
        out_shape=[
            jax.ShapeDtypeStruct((length, DIN), BF16),
            jax.ShapeDtypeStruct((PAIRS, length, 2), F32),
            jax.ShapeDtypeStruct((PAIRS, 2, length), F32),
            jax.ShapeDtypeStruct((PAIRS, 1, 2 * P_SIZE), F32),
            jax.ShapeDtypeStruct((length, 2 * N), F32),
        ],
        scratch_shapes=[pltpu.VMEM((length, length), F32)] * 3,
        cost_estimate=pl.CostEstimate(
            flops=4 * H * length * length * 2 * P_SIZE,
            bytes_accessed=8 * length * DIN,
            transcendentals=H * length * length,
        ),
        name="core",
    )(
        activated, dy, activated, pair_col(cum), cumr, pair_col(step),
        docs[:, None], docs[None, :], skip_wide.reshape(PAIRS, 1, 2 * P_SIZE),
    )
    back = lambda v: v.transpose(1, 0, 2).reshape(length, H)
    return dx, back(xdx), col.reshape(H, length).T, xdy, dbc


def scan_kernel(parts_ref, decay_ref, out_ref):
    count = parts_ref.shape[0]
    zero = jnp.zeros(parts_ref.shape[1:], F32)
    rows = parts_ref.shape[1] // 2
    forward = zero[:rows]
    for b in range(count):
        out_ref[b, :rows] = forward.astype(BF16)
        forward = decay_ref[b : b + 1] * forward + parts_ref[b, :rows].astype(F32)
    backward = zero[:rows]
    for b in reversed(range(count)):
        out_ref[b, rows:] = backward.astype(BF16)
        backward = decay_ref[b : b + 1] * backward + parts_ref[b, rows:].astype(F32)


def per_device(xbc, dt_raw, conv_weight, conv_bias, dt_bias, a_log, d_skip, grad_out, doc_lengths):
    taps = conv_weight.shape[0]
    own_rows = xbc[0]
    length = own_rows.shape[0]
    count = lax.axis_size("ctx")
    dy = grad_out[0]
    expand = jnp.asarray(np.kron(np.eye(H), np.ones((1, P_SIZE))), F32)
    widen = lambda v: dot(v, expand, 1, 0, HIGHEST)
    narrow = lambda v: dot(v, expand, 1, 1, HIGHEST)
    upto = jnp.tril(jnp.ones((length, length), F32))

    offset = lax.axis_index("ctx") * length
    positions = offset + jnp.arange(length + taps - 1, dtype=jnp.int32) - (taps - 1)
    docs_ext = doc_index(doc_lengths[0], positions)
    docs = docs_ext[taps - 1 :]
    prev_doc = docs_ext[taps - 2]
    rim_rows = from_behind(own_rows[length - taps + 1 :], "ctx", 1)
    extended = jnp.concatenate([rim_rows, own_rows], axis=0)
    keeps = [(docs_ext[k : k + length] == docs)[:, None] for k in range(taps)]
    shifted = [
        jnp.where(keeps[k], extended[k : k + length].astype(F32), 0.0) for k in range(taps)
    ]
    pre = conv_bias[None, :]
    for k in range(taps):
        pre = pre + conv_weight[k][None, :] * shifted[k]
    activated = jax.nn.silu(pre).astype(BF16)
    x = activated[:, :DIN].astype(F32)
    b, c = activated[:, DIN : DIN + N], activated[:, DIN + N :]

    raw = dt_raw[0].astype(F32) + dt_bias[None, :]
    step = jax.nn.softplus(raw)
    rate = -jnp.exp(a_log)
    cum = dot(upto, step * rate[None, :], 1, 0, HIGHEST)
    same_last = (docs == docs[-1]).astype(F32)[:, None]
    tail = jnp.exp(cum[-1][None, :] - cum) * same_last * step
    lead = jnp.exp(cum) * (docs == prev_doc).astype(F32)[:, None]
    decay = jnp.exp(cum[-1]) * (docs[-1] == prev_doc).astype(F32)
    tail_wide = widen(tail)
    weighted = (x * tail_wide).astype(BF16)
    led = (dy.astype(F32) * widen(lead)).astype(BF16)
    local = dot(b, weighted, 0, 0)
    seeded = dot(c, led, 0, 0)

    rows = N // count
    parts = jnp.concatenate(
        [local.reshape(count, rows, DIN), seeded.reshape(count, rows, DIN)], axis=1
    ).astype(BF16)
    parts = lax.all_to_all(parts, "ctx", 0, 0, tiled=True)
    decays = widen(lax.all_gather(decay, "ctx"))
    carried = pl.pallas_call(
        scan_kernel, out_shape=jax.ShapeDtypeStruct(parts.shape, BF16), name="carry"
    )(parts, decays)
    carried = lax.all_to_all(carried, "ctx", 0, 0, tiled=True)
    incoming = carried[:, :rows].reshape(N, DIN)
    adjoint = carried[:, rows:].reshape(N, DIN)

    dx, xdx, col, xdy, dbc = core(activated, dy, cum, step, docs, jnp.repeat(d_skip, P_SIZE))
    outer = dot(c, incoming, 1, 0)
    spread = dot(b, adjoint, 1, 0)
    from_lead = narrow(led.astype(F32) * outer)
    from_tail = narrow(spread * weighted.astype(F32))
    db = dbc[:, :N] + dot(weighted, adjoint, 1, 1)
    dc = dbc[:, N:] + dot(led, incoming, 1, 1)
    grad_act = jnp.concatenate([dx.astype(F32) + spread * tail_wide, db, dc], axis=1)
    grad_act = grad_act.astype(BF16).astype(F32)

    met = jnp.sum(adjoint.astype(F32) * incoming.astype(F32), axis=0, keepdims=True)
    grad_last = jnp.sum(from_tail, axis=0) + narrow(met)[0] * decay
    grad_cum = col - xdx + from_lead - from_tail
    grad_scaled = dot(upto, grad_cum, 0, 0, HIGHEST) + grad_last[None, :]
    grad_step = (xdx + from_tail) / step + grad_scaled * rate[None, :]
    grad_alog = jnp.sum(grad_scaled * step, axis=0) * rate
    grad_raw = grad_step * jax.nn.sigmoid(raw)
    grad_raw16 = grad_raw.astype(BF16)
    grad_dtb = jnp.sum(grad_raw, axis=0)
    grad_skip = jnp.sum(xdy.reshape(H, P_SIZE), axis=1)

    gate = jax.nn.sigmoid(pre)
    grad_pre = grad_act * (gate * (1.0 + pre * (1.0 - gate)))
    grad_weight = jnp.stack([jnp.sum(grad_pre * shifted[k], axis=0) for k in range(taps)])
    grad_bias = jnp.sum(grad_pre, axis=0)
    grad_ext = 0.0
    for k in range(taps):
        term = jnp.where(keeps[k], conv_weight[k][None, :] * grad_pre, 0.0)
        grad_ext = grad_ext + jnp.pad(term, ((k, taps - 1 - k), (0, 0)))
    grad_ext = grad_ext.astype(BF16)
    returned = from_behind(grad_ext[: taps - 1], "ctx", -1).astype(F32)
    own_grad = grad_ext[taps - 1 :].astype(F32)
    own_grad = own_grad + jnp.pad(returned, ((length - taps + 1, 0), (0, 0)))
    sums = lax.psum((grad_weight, grad_bias, grad_dtb, grad_alog, grad_skip), ("ctx", "bal"))
    return (own_grad.astype(BF16)[None], grad_raw16[None], *sums)


def solution(mesh):
    in_specs = (
        P("bal", "ctx", None),
        P("bal", "ctx", None),
        P(),
        P(),
        P(),
        P(),
        P(),
        P("bal", "ctx", None),
        P("bal", None),
    )
    out_specs = (P("bal", "ctx", None), P("bal", "ctx", None), P(), P(), P(), P(), P())
    return jax.shard_map(
        per_device, mesh=mesh, in_specs=in_specs, out_specs=out_specs, check_vma=False
    )
```

```python
import jax
import jax.numpy as jnp
import numpy as np
from jax import lax
from jax.experimental import pallas as pl
from jax.experimental.pallas import tpu as pltpu
from jax.sharding import PartitionSpec as P

H = 40
P_SIZE = 64
N = 64
DIN = H * P_SIZE
PAIRS = H // 2
HIGHEST = lax.Precision.HIGHEST
F32 = jnp.float32
BF16 = jnp.bfloat16


def from_behind(value, axis, steps):
    count = lax.axis_size(axis)
    leading, last = (max(0, -steps), min(count, count - steps))
    return lax.ppermute(value, axis, [(source, source + steps) for source in range(leading, last)])


def doc_index(lengths, positions):
    starts = jnp.cumsum(lengths) - lengths
    hits = (positions[:, None] >= starts[None, :]).astype(jnp.int32)
    return jnp.sum(hits, axis=1) - 1


def dot(a, b, ca, cb, precision=None):
    return lax.dot_general(
        a, b, (((ca,), (cb,)), ((), ())), precision=precision, preferred_element_type=F32
    )


def core_kernel(
    x_ref, dy_ref, bc_ref, steps_ref, docc_ref, docr_ref, skip_ref,
    dx_ref, rows_ref, xdy_ref, dbc_ref,
    scores, masked, gacc,
):
    j = pl.program_id(0)
    length = x_ref.shape[0]

    @pl.when(j == 0)
    def _():
        b, c = bc_ref[:, :N], bc_ref[:, N:]
        scores[...] = dot(b, c, 1, 1)
        s = lax.broadcasted_iota(jnp.int32, (length, length), 0)
        t = lax.broadcasted_iota(jnp.int32, (length, length), 1)
        same = (docc_ref[...] == docr_ref[...]) & (t >= s)
        masked[...] = jnp.where(same, 0.0, -1e30)
        gacc[...] = jnp.zeros_like(gacc)

    x, dy = x_ref[...], dy_ref[...]
    lane = lax.broadcasted_iota(jnp.int32, (length, 2 * P_SIZE), 1)
    rows = steps_ref[0]
    cols = rows.T
    mixes = []
    total = None
    for h in range(2):
        xh = jnp.where((lane < P_SIZE) == (h == 0), x, jnp.zeros_like(x))
        dw = dot(xh, dy, 1, 1)
        gap = rows[h : h + 1, :] - cols[:, h : h + 1]
        ds = jnp.exp(jnp.minimum(gap, 0.0) + masked[...]) * cols[:, h + 2 : h + 3]
        w = ds * scores[...]
        part = dw * ds
        total = part if total is None else total + part
        rows_ref[0, h + 2 : h + 3, :] = jnp.sum(dw * w, axis=0, keepdims=True)
        mixes.append(dot(w.astype(BF16), dy, 1, 0))
    gacc[...] += total
    mix = jnp.where(lane < P_SIZE, mixes[0], mixes[1])
    xf, dyf = x.astype(F32), dy.astype(F32)
    xm = xf * mix
    high = xm.astype(BF16)
    low = (xm - high.astype(F32)).astype(BF16)
    head = lax.broadcasted_iota(jnp.int32, (8, 2 * P_SIZE), 0)
    pick = lax.broadcasted_iota(jnp.int32, (8, 2 * P_SIZE), 1) // P_SIZE == head
    pick = jnp.where(pick, 1.0, 0.0).astype(BF16)
    rows_ref[0, :2, :] = (dot(pick, high, 1, 1) + dot(pick, low, 1, 1))[:2]
    xdy_ref[0] = jnp.sum(xf * dyf, axis=0, keepdims=True)
    dx_ref[...] = (mix + skip_ref[0] * dyf).astype(BF16)

    @pl.when(j == PAIRS - 1)
    def _():
        b, c = bc_ref[:, :N], bc_ref[:, N:]
        g = gacc[...].astype(BF16)
        dbc_ref[:, :N] = dot(g, c, 1, 0)
        dbc_ref[:, N:] = dot(g, b, 0, 0)


def core(activated, dy, cum, step, docs, skip_wide):
    length = activated.shape[0]
    pairs = lambda v: v.reshape(PAIRS, 2, length)
    packed = jnp.concatenate(
        [pairs(cum), pairs(step), jnp.zeros((PAIRS, 4, length), F32)], axis=1
    )
    wide = pl.BlockSpec((length, 2 * P_SIZE), lambda j: (0, j))
    lanes = pl.BlockSpec((1, 1, 2 * P_SIZE), lambda j: (j, 0, 0))
    dx, rows, xdy, dbc = pl.pallas_call(
        core_kernel,
        grid=(PAIRS,),
        in_specs=[
            wide,
            wide,
            pl.BlockSpec((length, 2 * N), lambda j: (0, PAIRS)),
            pl.BlockSpec((1, 8, length), lambda j: (j, 0, 0)),
            pl.BlockSpec((length, 1), lambda j: (0, 0)),
            pl.BlockSpec((1, length), lambda j: (0, 0)),
            lanes,
        ],
        out_specs=[
            wide,
            pl.BlockSpec((1, 4, length), lambda j: (j, 0, 0)),
            lanes,
            pl.BlockSpec((length, 2 * N), lambda j: (0, 0)),
        ],
        out_shape=[
            jax.ShapeDtypeStruct((length, DIN), BF16),
            jax.ShapeDtypeStruct((PAIRS, 4, length), F32),
            jax.ShapeDtypeStruct((PAIRS, 1, 2 * P_SIZE), F32),
            jax.ShapeDtypeStruct((length, 2 * N), F32),
        ],
        scratch_shapes=[pltpu.VMEM((length, length), F32)] * 3,
        cost_estimate=pl.CostEstimate(
            flops=4 * H * length * length * 2 * P_SIZE,
            bytes_accessed=8 * length * DIN,
            transcendentals=H * length * length,
        ),
        name="core",
    )(
        activated, dy, activated, packed,
        docs[:, None], docs[None, :], skip_wide.reshape(PAIRS, 1, 2 * P_SIZE),
    )
    xdx, col = rows[:, :2].reshape(H, length), rows[:, 2:].reshape(H, length)
    return dx, xdx, col, xdy, dbc


def total_kernel(
    v_ref, out_ref, got, mid, across, last, spread,
    send_a, recv_a, send_b, recv_b, send_c, recv_c,
):
    nc, nb = lax.axis_size("ctx"), lax.axis_size("bal")
    ctx, bal = lax.axis_index("ctx"), lax.axis_index("bal")

    def to_ctx(k):
        return lax.rem(ctx + k, nc)

    def to_bal(k):
        return lax.rem(bal + k, nb)

    def send(src, dst, sends, recvs, axis, peer, k):
        return pltpu.make_async_remote_copy(
            src_ref=src, dst_ref=dst, send_sem=sends.at[k], recv_sem=recvs.at[k],
            device_id={axis: peer}, device_id_type=pl.DeviceIdType.MESH,
        )

    barrier = pltpu.get_barrier_semaphore()

    @pl.loop(1, nc)
    def _(k):
        pl.semaphore_signal(
            barrier, 1, device_id={"ctx": to_ctx(k)}, device_id_type=pl.DeviceIdType.MESH
        )

    @pl.loop(1, nb)
    def _(k):
        pl.semaphore_signal(
            barrier, 1, device_id={"bal": to_bal(k)}, device_id_type=pl.DeviceIdType.MESH
        )

    pl.semaphore_wait(barrier, nc + nb - 2)

    def first(k):
        return send(v_ref.at[to_ctx(k)], got.at[k], send_a, recv_a, "ctx", to_ctx(k), k)

    def second(k):
        return send(mid, across.at[bal], send_b, recv_b, "bal", to_bal(k), k)

    def third(k):
        return send(last, spread.at[ctx], send_c, recv_c, "ctx", to_ctx(k), k)

    @pl.loop(1, nc)
    def _(k):
        first(k).start()

    got[0] = v_ref[ctx]

    @pl.loop(1, nc)
    def _(k):
        first(k).wait()

    summed = jnp.sum(got[...], axis=0)
    mid[...] = summed
    across[bal] = summed

    @pl.loop(1, nb)
    def _(k):
        second(k).start()

    @pl.loop(1, nb)
    def _(k):
        second(k).wait()

    summed = jnp.sum(across[...], axis=0)
    last[...] = summed
    spread[ctx] = summed

    @pl.loop(1, nc)
    def _(k):
        third(k).start()

    @pl.loop(1, nc)
    def _(k):
        third(k).wait()

    out_ref[...] = spread[...]


def total_sum(vector):
    nc, nb = lax.axis_size("ctx"), lax.axis_size("bal")
    rows = -(-vector.shape[0] // (nc * 128))
    padded = jnp.pad(vector, (0, nc * rows * 128 - vector.shape[0])).reshape(nc, rows, 128)
    dma = pltpu.SemaphoreType.DMA
    summed = pl.pallas_call(
        total_kernel,
        out_shape=jax.ShapeDtypeStruct(padded.shape, F32),
        in_specs=[pl.BlockSpec(memory_space=pltpu.VMEM)],
        out_specs=pl.BlockSpec(memory_space=pltpu.VMEM),
        scratch_shapes=[
            pltpu.VMEM((nc, rows, 128), F32),
            pltpu.VMEM((rows, 128), F32),
            pltpu.VMEM((nb, rows, 128), F32),
            pltpu.VMEM((rows, 128), F32),
            pltpu.VMEM((nc, rows, 128), F32),
            dma((nc,)), dma((nc,)), dma((nb,)), dma((nb,)), dma((nc,)), dma((nc,)),
        ],
        compiler_params=pltpu.CompilerParams(collective_id=0, has_side_effects=True),
        name="total",
    )(padded)
    return summed.reshape(-1)[: vector.shape[0]]


def exchange_kernel(
    parts_ref, decay_ref, out_ref, got, decays, turned, result,
    send_a, recv_a, send_d, recv_d, send_b, recv_b,
):
    nc = lax.axis_size("ctx")
    ctx = lax.axis_index("ctx")
    rows = parts_ref.shape[1] // 2

    def peer(k):
        return lax.rem(ctx + k, nc)

    def send(src, dst, sends, recvs, k):
        return pltpu.make_async_remote_copy(
            src_ref=src, dst_ref=dst, send_sem=sends.at[k], recv_sem=recvs.at[k],
            device_id={"ctx": peer(k)}, device_id_type=pl.DeviceIdType.MESH,
        )

    def both_ways(i):
        half = (i + 1) // 2
        return jnp.where(lax.rem(i, 2) == 1, half, nc - half)

    barrier = pltpu.get_barrier_semaphore()

    @pl.loop(1, nc)
    def _(k):
        pl.semaphore_signal(
            barrier, 1, device_id={"ctx": peer(k)}, device_id_type=pl.DeviceIdType.MESH
        )

    pl.semaphore_wait(barrier, nc - 1)

    def small(k):
        return send(decay_ref, decays.at[ctx], send_d, recv_d, k)

    def out(k):
        return send(parts_ref.at[peer(k)], got.at[ctx], send_a, recv_a, k)

    def back(k):
        return send(turned.at[peer(k)], result.at[ctx], send_b, recv_b, k)

    @pl.loop(1, nc)
    def _(i):
        small(both_ways(i)).start()
        out(both_ways(i)).start()

    decays[ctx] = decay_ref[...]
    got[ctx] = parts_ref[ctx]

    @pl.loop(1, nc)
    def _(k):
        small(k).wait()
        out(k).wait()

    shape = (128, parts_ref.shape[2])
    head = lax.broadcasted_iota(jnp.int32, shape, 1) // P_SIZE
    own = head == lax.broadcasted_iota(jnp.int32, shape, 0)
    decay = dot(decays[:, 0, :], jnp.where(own, 1.0, 0.0), 1, 0, HIGHEST)
    forward = jnp.zeros((rows, parts_ref.shape[2]), F32)
    for b in range(nc):
        turned[b, :rows] = forward.astype(BF16)
        forward = decay[b : b + 1] * forward + got[b, :rows].astype(F32)
    backward = jnp.zeros((rows, parts_ref.shape[2]), F32)
    for b in reversed(range(nc)):
        turned[b, rows:] = backward.astype(BF16)
        backward = decay[b : b + 1] * backward + got[b, rows:].astype(F32)

    @pl.loop(1, nc)
    def _(i):
        back(both_ways(i)).start()

    result[ctx] = turned[ctx]

    @pl.loop(1, nc)
    def _(k):
        back(k).wait()

    out_ref[...] = result[...]


def exchange(parts, decay):
    nc = parts.shape[0]
    dma = pltpu.SemaphoreType.DMA
    return pl.pallas_call(
        exchange_kernel,
        out_shape=jax.ShapeDtypeStruct(parts.shape, BF16),
        in_specs=[pl.BlockSpec(memory_space=pltpu.VMEM)] * 2,
        out_specs=pl.BlockSpec(memory_space=pltpu.VMEM),
        scratch_shapes=[
            pltpu.VMEM(parts.shape, BF16),
            pltpu.VMEM((nc, 1, 128), F32),
            pltpu.VMEM(parts.shape, BF16),
            pltpu.VMEM(parts.shape, BF16),
            *[dma((nc,))] * 6,
        ],
        compiler_params=pltpu.CompilerParams(collective_id=1, has_side_effects=True),
        name="exchange",
    )(parts, jnp.pad(decay, (0, 128 - H))[None, :])


def per_device(xbc, dt_raw, conv_weight, conv_bias, dt_bias, a_log, d_skip, grad_out, doc_lengths):
    taps = conv_weight.shape[0]
    own_rows = xbc[0]
    length = own_rows.shape[0]
    count = lax.axis_size("ctx")
    dy = grad_out[0]
    expand = jnp.asarray(np.kron(np.eye(H), np.ones((1, P_SIZE))), F32)
    widen = lambda v: dot(v, expand, 0, 0, HIGHEST)
    narrow = lambda v: dot(expand, v, 1, 1, HIGHEST)
    upto = jnp.triu(jnp.ones((length, length), F32))

    offset = lax.axis_index("ctx") * length
    positions = offset + jnp.arange(length + taps - 1, dtype=jnp.int32) - (taps - 1)
    docs_ext = doc_index(doc_lengths[0], positions)
    docs = docs_ext[taps - 1 :]
    prev_doc = docs_ext[taps - 2]
    rim_rows = from_behind(own_rows[length - taps + 1 :], "ctx", 1)
    extended = jnp.concatenate([rim_rows, own_rows], axis=0)
    keeps = [(docs_ext[k : k + length] == docs)[:, None] for k in range(taps)]
    shifted = [
        jnp.where(keeps[k], extended[k : k + length].astype(F32), 0.0) for k in range(taps)
    ]
    pre = conv_bias[None, :]
    for k in range(taps):
        pre = pre + conv_weight[k][None, :] * shifted[k]
    activated = jax.nn.silu(pre).astype(BF16)
    x = activated[:, :DIN].astype(F32)
    b, c = activated[:, DIN : DIN + N], activated[:, DIN + N :]

    raw = dt_raw[0].T.astype(F32) + dt_bias[:, None]
    step = jax.nn.softplus(raw)
    rate = -jnp.exp(a_log)[:, None]
    cum = dot(step * rate, upto, 1, 0, HIGHEST)
    same_last = (docs == docs[-1]).astype(F32)[None, :]
    tail = jnp.exp(cum[:, -1:] - cum) * same_last * step
    lead = jnp.exp(cum) * (docs == prev_doc).astype(F32)[None, :]
    decay = jnp.exp(cum[:, -1]) * (docs[-1] == prev_doc).astype(F32)
    tail_wide = widen(tail)
    weighted = (x * tail_wide).astype(BF16)
    led = (dy.astype(F32) * widen(lead)).astype(BF16)
    local = dot(b, weighted, 0, 0)
    seeded = dot(c, led, 0, 0)

    rows = N // count
    parts = jnp.concatenate(
        [local.reshape(count, rows, DIN), seeded.reshape(count, rows, DIN)], axis=1
    ).astype(BF16)
    carried = exchange(parts, decay)
    incoming = carried[:, :rows].reshape(N, DIN)
    adjoint = carried[:, rows:].reshape(N, DIN)

    dx, xdx, col, xdy, dbc = core(activated, dy, cum, step, docs, jnp.repeat(d_skip, P_SIZE))
    outer = dot(c, incoming, 1, 0)
    spread = dot(b, adjoint, 1, 0)
    from_lead = narrow(led.astype(F32) * outer)
    from_tail = narrow(spread * weighted.astype(F32))
    db = dbc[:, :N] + dot(weighted, adjoint, 1, 1)
    dc = dbc[:, N:] + dot(led, incoming, 1, 1)
    grad_act = jnp.concatenate([dx.astype(F32) + spread * tail_wide, db, dc], axis=1)
    grad_act = grad_act.astype(BF16).astype(F32)

    met = jnp.sum(adjoint.astype(F32) * incoming.astype(F32), axis=0, keepdims=True)
    grad_last = jnp.sum(from_tail, axis=1, keepdims=True) + narrow(met) * decay[:, None]
    grad_cum = col - xdx + from_lead - from_tail
    grad_scaled = dot(grad_cum, upto, 1, 1, HIGHEST) + grad_last
    grad_step = (xdx + from_tail) / step + grad_scaled * rate
    grad_alog = jnp.sum(grad_scaled * step, axis=1) * rate[:, 0]
    grad_raw = grad_step * jax.nn.sigmoid(raw)
    grad_raw16 = grad_raw.astype(BF16).T
    grad_dtb = jnp.sum(grad_raw, axis=1)
    grad_skip = jnp.sum(xdy.reshape(H, P_SIZE), axis=1)

    gate = jax.nn.sigmoid(pre)
    grad_pre = grad_act * (gate * (1.0 + pre * (1.0 - gate)))
    grad_weight = jnp.stack([jnp.sum(grad_pre * shifted[k], axis=0) for k in range(taps)])
    grad_bias = jnp.sum(grad_pre, axis=0)
    grad_ext = 0.0
    for k in range(taps):
        term = jnp.where(keeps[k], conv_weight[k][None, :] * grad_pre, 0.0)
        grad_ext = grad_ext + jnp.pad(term, ((k, taps - 1 - k), (0, 0)))
    grad_ext = grad_ext.astype(BF16)
    returned = from_behind(grad_ext[: taps - 1], "ctx", -1).astype(F32)
    own_grad = grad_ext[taps - 1 :].astype(F32)
    own_grad = own_grad + jnp.pad(returned, ((length - taps + 1, 0), (0, 0)))
    mine = (grad_weight, grad_bias, grad_dtb, grad_alog, grad_skip)
    total = total_sum(jnp.concatenate([part.reshape(-1) for part in mine]))
    ends = np.cumsum([part.size for part in mine])[:-1].tolist()
    sums = [part.reshape(like.shape) for part, like in zip(jnp.split(total, ends), mine)]
    return (own_grad.astype(BF16)[None], grad_raw16[None], *sums)


def solution(mesh):
    in_specs = (
        P("bal", "ctx", None),
        P("bal", "ctx", None),
        P(),
        P(),
        P(),
        P(),
        P(),
        P("bal", "ctx", None),
        P("bal", None),
    )
    out_specs = (P("bal", "ctx", None), P("bal", "ctx", None), P(), P(), P(), P(), P())
    return jax.shard_map(
        per_device, mesh=mesh, in_specs=in_specs, out_specs=out_specs, check_vma=False
    )
```

```python
import jax
import jax.numpy as jnp
import numpy as np
from jax import lax
from jax.experimental import pallas as pl
from jax.experimental.pallas import tpu as pltpu
from jax.sharding import PartitionSpec as P

H = 40
P_SIZE = 64
N = 64
DIN = H * P_SIZE
PAIRS = H // 2
EARLY, MIDDLE = 3, 12
HIGHEST = lax.Precision.HIGHEST
F32 = jnp.float32
BF16 = jnp.bfloat16


def from_behind(value, axis, steps):
    count = lax.axis_size(axis)
    leading, last = (max(0, -steps), min(count, count - steps))
    return lax.ppermute(value, axis, [(source, source + steps) for source in range(leading, last)])


def doc_index(lengths, positions):
    starts = jnp.cumsum(lengths) - lengths
    hits = (positions[:, None] >= starts[None, :]).astype(jnp.int32)
    return jnp.sum(hits, axis=1) - 1


def dot(a, b, ca, cb, precision=None):
    return lax.dot_general(
        a, b, (((ca,), (cb,)), ((), ())), precision=precision, preferred_element_type=F32
    )


def core_pair(j, x_ref, dy_ref, steps_ref, skip_ref, dx_ref, rows_ref, xdy_ref, scores, masked, gacc):
    length = x_ref.shape[0]
    where = pl.ds(pl.multiple_of(j * 2 * P_SIZE, 2 * P_SIZE), 2 * P_SIZE)
    x, dy = x_ref[:, where], dy_ref[:, where]
    lane = lax.broadcasted_iota(jnp.int32, (length, 2 * P_SIZE), 1)
    rows = steps_ref[j]
    cols = rows.T
    mixes = []
    total = None
    for h in range(2):
        xh = jnp.where((lane < P_SIZE) == (h == 0), x, jnp.zeros_like(x))
        dw = dot(xh, dy, 1, 1)
        gap = rows[h : h + 1, :] - cols[:, h : h + 1]
        ds = jnp.exp(jnp.minimum(gap, 0.0) + masked[...]) * cols[:, h + 2 : h + 3]
        w = ds * scores[...]
        part = dw * ds
        total = part if total is None else total + part
        rows_ref[j, h + 2 : h + 3, :] = jnp.sum(dw * w, axis=0, keepdims=True)
        mixes.append(dot(w.astype(BF16), dy, 1, 0))
    gacc[...] += total
    mix = jnp.where(lane < P_SIZE, mixes[0], mixes[1])
    xf, dyf = x.astype(F32), dy.astype(F32)
    xm = xf * mix
    high = xm.astype(BF16)
    low = (xm - high.astype(F32)).astype(BF16)
    head = lax.broadcasted_iota(jnp.int32, (8, 2 * P_SIZE), 0)
    pick = lax.broadcasted_iota(jnp.int32, (8, 2 * P_SIZE), 1) // P_SIZE == head
    pick = jnp.where(pick, 1.0, 0.0).astype(BF16)
    rows_ref[j, :2, :] = (dot(pick, high, 1, 1) + dot(pick, low, 1, 1))[:2]
    xdy_ref[j] = jnp.sum(xf * dyf, axis=0, keepdims=True)
    dx_ref[:, where] = (mix + skip_ref[j] * dyf).astype(BF16)


def core_kernel(
    x_ref, dy_ref, steps_ref, docc_ref, docr_ref, skip_ref, parts_ref, decay_ref,
    dx_ref, rows_ref, xdy_ref, dbc_ref, out_ref,
    scores, masked, gacc,
    other, theirs, comb, chain, got, chains, turned, result, lend, landed,
    pair_sems, send_a, recv_a, send_d, recv_d, send_b, recv_b,
):
    length = x_ref.shape[0]
    nc = lax.axis_size("ctx")
    chips = nc // 2
    ctx = lax.axis_index("ctx")
    chip, side = ctx // 2, lax.rem(ctx, 2)
    partner = chip * 2 + 1 - side
    mesh = pl.DeviceIdType.MESH
    rows = parts_ref.shape[2] // 2

    def target(k):
        return lax.rem(chip + k, chips)

    def peer(k):
        return target(k) * 2 + side

    def send(src, dst, sends, recvs, k):
        return pltpu.make_async_remote_copy(
            src_ref=src, dst_ref=dst, send_sem=sends.at[k], recv_sem=recvs.at[k],
            device_id={"ctx": peer(k)}, device_id_type=mesh,
        )

    def swap(src, dst, i):
        return pltpu.make_async_remote_copy(
            src_ref=src, dst_ref=dst, send_sem=pair_sems.at[2 * i], recv_sem=pair_sems.at[2 * i + 1],
            device_id={"ctx": partner}, device_id_type=mesh,
        )

    def both_ways(i):
        half = (i + 1) // 2
        return jnp.where(lax.rem(i, 2) == 1, half, chips - half)

    def pairs(start, stop):
        @pl.loop(start, stop)
        def _(j):
            core_pair(
                j, x_ref, dy_ref, steps_ref, skip_ref, dx_ref, rows_ref, xdy_ref,
                scores, masked, gacc,
            )

    barrier = pltpu.get_barrier_semaphore()
    pl.semaphore_signal(barrier, 1, device_id={"ctx": partner}, device_id_type=mesh)

    @pl.loop(1, chips)
    def _(k):
        pl.semaphore_signal(barrier, 1, device_id={"ctx": peer(k)}, device_id_type=mesh)

    b, c = x_ref[:, DIN : DIN + N], x_ref[:, DIN + N :]
    scores[...] = dot(b, c, 1, 1)
    s = lax.broadcasted_iota(jnp.int32, (length, length), 0)
    t = lax.broadcasted_iota(jnp.int32, (length, length), 1)
    same = (docc_ref[...] == docr_ref[...]) & (t >= s)
    masked[...] = jnp.where(same, 0.0, -1e30)
    gacc[...] = jnp.zeros_like(gacc)
    pairs(0, EARLY)
    pl.semaphore_wait(barrier, chips)

    gives = swap(parts_ref.at[1 - side], other, 0)
    tells = swap(decay_ref, theirs, 1)
    gives.start()
    tells.start()
    gives.wait()
    tells.wait()

    shape = (128, parts_ref.shape[3])
    head = lax.broadcasted_iota(jnp.int32, shape, 1) // P_SIZE + side * (H // 2)
    own = jnp.where(head == lax.broadcasted_iota(jnp.int32, shape, 0), 1.0, 0.0)
    mine, yours = decay_ref[...], theirs[...]
    stacked = jnp.concatenate([jnp.broadcast_to(mine, (8, 128)), jnp.broadcast_to(yours, (8, 128))])
    spread = dot(stacked, own, 1, 0, HIGHEST)
    mine_wide, yours_wide = spread[:8], spread[8:]
    is_forward = lax.broadcasted_iota(jnp.int32, (2 * rows, shape[1]), 0) < rows
    keep_other = is_forward == (side == 0)
    own_gain = jnp.where(keep_other, yours_wide, 1.0)
    other_gain = jnp.where(keep_other, 1.0, mine_wide)
    for i in range(chips):
        comb[i] = (
            own_gain * parts_ref[side, i].astype(F32) + other_gain * other[i].astype(F32)
        ).astype(BF16)
    chain[...] = mine * yours

    def out(k):
        return send(comb.at[target(k)], got.at[chip], send_a, recv_a, k)

    def small(k):
        return send(chain, chains.at[chip], send_d, recv_d, k)

    def back(k):
        return send(turned.at[target(k)], result.at[chip], send_b, recv_b, k)

    @pl.loop(1, chips)
    def _(i):
        small(both_ways(i)).start()
        out(both_ways(i)).start()

    got[chip] = comb[chip]
    chains[chip] = chain[...]
    pairs(EARLY, MIDDLE)

    @pl.loop(1, chips)
    def _(k):
        small(k).wait()
        out(k).wait()

    decay = dot(chains[:, 0, :], own, 1, 0, HIGHEST)
    forward = jnp.zeros((rows, shape[1]), F32)
    for i in range(chips):
        turned[i, :rows] = forward.astype(BF16)
        forward = decay[i : i + 1] * forward + got[i, :rows].astype(F32)
    backward = jnp.zeros((rows, shape[1]), F32)
    for i in reversed(range(chips)):
        turned[i, rows:] = backward.astype(BF16)
        backward = decay[i : i + 1] * backward + got[i, rows:].astype(F32)

    @pl.loop(1, chips)
    def _(i):
        back(both_ways(i)).start()

    result[chip] = turned[chip]
    pairs(MIDDLE, PAIRS)
    g = gacc[...].astype(BF16)
    dbc_ref[:, :N] = dot(g, c, 1, 0)
    dbc_ref[:, N:] = dot(g, b, 0, 0)

    @pl.loop(1, chips)
    def _(k):
        back(k).wait()

    for i in range(chips):
        value = result[i].astype(F32)
        here = jnp.where(keep_other, 1.0, yours_wide) * value
        here = here + jnp.where(keep_other, 0.0, other[i].astype(F32))
        there = jnp.where(keep_other, mine_wide, 1.0) * value
        there = there + jnp.where(keep_other, parts_ref[side, i].astype(F32), 0.0)
        out_ref[side, i] = here.astype(BF16)
        lend[i] = there.astype(BF16)
    lends = swap(lend, landed, 2)
    lends.start()
    lends.wait()
    out_ref[1 - side] = landed[...]


def core(activated, dy, cum, step, docs, skip_wide, parts, decay):
    length = activated.shape[0]
    chips = parts.shape[1]
    pairs = lambda v: v.reshape(PAIRS, 2, length)
    packed = jnp.concatenate(
        [pairs(cum), pairs(step), jnp.zeros((PAIRS, 4, length), F32)], axis=1
    )
    vmem = pl.BlockSpec(memory_space=pltpu.VMEM)
    dma = pltpu.SemaphoreType.DMA
    half = pltpu.VMEM(parts.shape[1:], BF16)
    line = pltpu.VMEM((1, 128), F32)
    dx, rows, xdy, dbc, carried = pl.pallas_call(
        core_kernel,
        in_specs=[vmem] * 8,
        out_specs=[vmem] * 5,
        out_shape=[
            jax.ShapeDtypeStruct((length, DIN), BF16),
            jax.ShapeDtypeStruct((PAIRS, 4, length), F32),
            jax.ShapeDtypeStruct((PAIRS, 1, 2 * P_SIZE), F32),
            jax.ShapeDtypeStruct((length, 2 * N), F32),
            jax.ShapeDtypeStruct(parts.shape, BF16),
        ],
        scratch_shapes=[
            *[pltpu.VMEM((length, length), F32)] * 3,
            half, line, half, line, half, pltpu.VMEM((chips, 1, 128), F32),
            half, half, half, half,
            dma((6,)), *[dma((chips,))] * 6,
        ],
        compiler_params=pltpu.CompilerParams(collective_id=1, has_side_effects=True),
        name="core",
    )(
        activated, dy, packed, docs[:, None], docs[None, :],
        skip_wide.reshape(PAIRS, 1, 2 * P_SIZE), parts,
        jnp.pad(decay, (0, 128 - H))[None, :],
    )
    xdx, col = rows[:, :2].reshape(H, length), rows[:, 2:].reshape(H, length)
    return dx, xdx, col, xdy, dbc, carried


def total_kernel(
    v_ref, out_ref, got, mid, across, last, spread,
    send_a, recv_a, send_b, recv_b, send_c, recv_c,
):
    nc, nb = lax.axis_size("ctx"), lax.axis_size("bal")
    ctx, bal = lax.axis_index("ctx"), lax.axis_index("bal")

    def to_ctx(k):
        return lax.rem(ctx + k, nc)

    def to_bal(k):
        return lax.rem(bal + k, nb)

    def send(src, dst, sends, recvs, axis, peer, k):
        return pltpu.make_async_remote_copy(
            src_ref=src, dst_ref=dst, send_sem=sends.at[k], recv_sem=recvs.at[k],
            device_id={axis: peer}, device_id_type=pl.DeviceIdType.MESH,
        )

    barrier = pltpu.get_barrier_semaphore()

    @pl.loop(1, nc)
    def _(k):
        pl.semaphore_signal(
            barrier, 1, device_id={"ctx": to_ctx(k)}, device_id_type=pl.DeviceIdType.MESH
        )

    @pl.loop(1, nb)
    def _(k):
        pl.semaphore_signal(
            barrier, 1, device_id={"bal": to_bal(k)}, device_id_type=pl.DeviceIdType.MESH
        )

    pl.semaphore_wait(barrier, nc + nb - 2)

    def first(k):
        return send(v_ref.at[to_ctx(k)], got.at[k], send_a, recv_a, "ctx", to_ctx(k), k)

    def second(k):
        return send(mid, across.at[bal], send_b, recv_b, "bal", to_bal(k), k)

    def third(k):
        return send(last, spread.at[ctx], send_c, recv_c, "ctx", to_ctx(k), k)

    @pl.loop(1, nc)
    def _(k):
        first(k).start()

    got[0] = v_ref[ctx]

    @pl.loop(1, nc)
    def _(k):
        first(k).wait()

    summed = jnp.sum(got[...], axis=0)
    mid[...] = summed
    across[bal] = summed

    @pl.loop(1, nb)
    def _(k):
        second(k).start()

    @pl.loop(1, nb)
    def _(k):
        second(k).wait()

    summed = jnp.sum(across[...], axis=0)
    last[...] = summed
    spread[ctx] = summed

    @pl.loop(1, nc)
    def _(k):
        third(k).start()

    @pl.loop(1, nc)
    def _(k):
        third(k).wait()

    out_ref[...] = spread[...]


def total_sum(vector):
    nc, nb = lax.axis_size("ctx"), lax.axis_size("bal")
    rows = -(-vector.shape[0] // (nc * 128))
    padded = jnp.pad(vector, (0, nc * rows * 128 - vector.shape[0])).reshape(nc, rows, 128)
    dma = pltpu.SemaphoreType.DMA
    summed = pl.pallas_call(
        total_kernel,
        out_shape=jax.ShapeDtypeStruct(padded.shape, F32),
        in_specs=[pl.BlockSpec(memory_space=pltpu.VMEM)],
        out_specs=pl.BlockSpec(memory_space=pltpu.VMEM),
        scratch_shapes=[
            pltpu.VMEM((nc, rows, 128), F32),
            pltpu.VMEM((rows, 128), F32),
            pltpu.VMEM((nb, rows, 128), F32),
            pltpu.VMEM((rows, 128), F32),
            pltpu.VMEM((nc, rows, 128), F32),
            dma((nc,)), dma((nc,)), dma((nb,)), dma((nb,)), dma((nc,)), dma((nc,)),
        ],
        compiler_params=pltpu.CompilerParams(collective_id=0, has_side_effects=True),
        name="total",
    )(padded)
    return summed.reshape(-1)[: vector.shape[0]]


def per_device(xbc, dt_raw, conv_weight, conv_bias, dt_bias, a_log, d_skip, grad_out, doc_lengths):
    taps = conv_weight.shape[0]
    own_rows = xbc[0]
    length = own_rows.shape[0]
    count = lax.axis_size("ctx")
    dy = grad_out[0]
    expand = jnp.asarray(np.kron(np.eye(H), np.ones((1, P_SIZE))), BF16)
    twice = jnp.concatenate([expand, expand])

    def halves(v):
        high = lax.reduce_precision(v, 8, 7)
        return high.astype(BF16), (v - high).astype(BF16)

    widen = lambda v: dot(jnp.concatenate(halves(v)), twice, 0, 0)
    narrow = lambda v: sum(dot(expand, part, 1, 1) for part in halves(v))
    upto = jnp.triu(jnp.ones((length, length), F32))

    offset = lax.axis_index("ctx") * length
    positions = offset + jnp.arange(length + taps - 1, dtype=jnp.int32) - (taps - 1)
    docs_ext = doc_index(doc_lengths[0], positions)
    docs = docs_ext[taps - 1 :]
    prev_doc = docs_ext[taps - 2]
    rim_rows = from_behind(own_rows[length - taps + 1 :], "ctx", 1)
    extended = jnp.concatenate([rim_rows, own_rows], axis=0)
    keeps = [(docs_ext[k : k + length] == docs)[:, None] for k in range(taps)]
    shifted = [
        jnp.where(keeps[k], extended[k : k + length].astype(F32), 0.0) for k in range(taps)
    ]
    pre = conv_bias[None, :]
    for k in range(taps):
        pre = pre + conv_weight[k][None, :] * shifted[k]
    activated = jax.nn.silu(pre).astype(BF16)
    x = activated[:, :DIN].astype(F32)
    b, c = activated[:, DIN : DIN + N], activated[:, DIN + N :]

    raw = dt_raw[0].T.astype(F32) + dt_bias[:, None]
    step = jax.nn.softplus(raw)
    rate = -jnp.exp(a_log)[:, None]
    cum = dot(step * rate, upto, 1, 0, HIGHEST)
    same_last = (docs == docs[-1]).astype(F32)[None, :]
    tail = jnp.exp(cum[:, -1:] - cum) * same_last * step
    lead = jnp.exp(cum) * (docs == prev_doc).astype(F32)[None, :]
    decay = jnp.exp(cum[:, -1]) * (docs[-1] == prev_doc).astype(F32)
    tail_wide = widen(tail)
    weighted = (x * tail_wide).astype(BF16)
    led = (dy.astype(F32) * widen(lead)).astype(BF16)
    local = dot(b, weighted, 0, 0)
    seeded = dot(c, led, 0, 0)

    chips = count // 2
    rows = N // chips
    split = lambda v: v.astype(BF16).reshape(chips, rows, 2, DIN // 2).transpose(2, 0, 1, 3)
    parts = jnp.concatenate([split(local), split(seeded)], axis=2)
    dx, xdx, col, xdy, dbc, carried = core(
        activated, dy, cum, step, docs, jnp.repeat(d_skip, P_SIZE), parts, decay
    )
    join = lambda v: v.transpose(1, 2, 0, 3).reshape(N, DIN)
    incoming, adjoint = join(carried[:, :, :rows]), join(carried[:, :, rows:])

    outer = dot(c, incoming, 1, 0)
    spread = dot(b, adjoint, 1, 0)
    from_lead = narrow(led.astype(F32) * outer)
    from_tail = narrow(spread * weighted.astype(F32))
    db = dbc[:, :N] + dot(weighted, adjoint, 1, 1)
    dc = dbc[:, N:] + dot(led, incoming, 1, 1)
    grad_act = jnp.concatenate([dx.astype(F32) + spread * tail_wide, db, dc], axis=1)
    grad_act = grad_act.astype(BF16).astype(F32)

    met = jnp.sum(adjoint.astype(F32) * incoming.astype(F32), axis=0, keepdims=True)
    grad_last = jnp.sum(from_tail, axis=1, keepdims=True) + narrow(met) * decay[:, None]
    grad_cum = col - xdx + from_lead - from_tail
    grad_scaled = dot(grad_cum, upto, 1, 1, HIGHEST) + grad_last
    grad_step = (xdx + from_tail) / step + grad_scaled * rate
    grad_alog = jnp.sum(grad_scaled * step, axis=1) * rate[:, 0]
    grad_raw = grad_step * jax.nn.sigmoid(raw)
    grad_raw16 = grad_raw.astype(BF16).T
    grad_dtb = jnp.sum(grad_raw, axis=1)
    grad_skip = jnp.sum(xdy.reshape(H, P_SIZE), axis=1)

    gate = jax.nn.sigmoid(pre)
    grad_pre = grad_act * (gate * (1.0 + pre * (1.0 - gate)))
    grad_weight = jnp.stack([jnp.sum(grad_pre * shifted[k], axis=0) for k in range(taps)])
    grad_bias = jnp.sum(grad_pre, axis=0)
    grad_ext = 0.0
    for k in range(taps):
        term = jnp.where(keeps[k], conv_weight[k][None, :] * grad_pre, 0.0)
        grad_ext = grad_ext + jnp.pad(term, ((k, taps - 1 - k), (0, 0)))
    grad_ext = grad_ext.astype(BF16)
    returned = from_behind(grad_ext[: taps - 1], "ctx", -1).astype(F32)
    own_grad = grad_ext[taps - 1 :].astype(F32)
    own_grad = own_grad + jnp.pad(returned, ((length - taps + 1, 0), (0, 0)))
    mine = (grad_weight, grad_bias, grad_dtb, grad_alog, grad_skip)
    total = total_sum(jnp.concatenate([part.reshape(-1) for part in mine]))
    ends = np.cumsum([part.size for part in mine])[:-1].tolist()
    sums = [part.reshape(like.shape) for part, like in zip(jnp.split(total, ends), mine)]
    return (own_grad.astype(BF16)[None], grad_raw16[None], *sums)


def solution(mesh):
    in_specs = (
        P("bal", "ctx", None),
        P("bal", "ctx", None),
        P(),
        P(),
        P(),
        P(),
        P(),
        P("bal", "ctx", None),
        P("bal", None),
    )
    out_specs = (P("bal", "ctx", None), P("bal", "ctx", None), P(), P(), P(), P(), P())
    return jax.shard_map(
        per_device, mesh=mesh, in_specs=in_specs, out_specs=out_specs, check_vma=False
    )
```

```python
import jax
import jax.numpy as jnp
import numpy as np
from jax import lax
from jax.experimental import pallas as pl
from jax.experimental.pallas import tpu as pltpu
from jax.sharding import PartitionSpec as P

H = 40
P_SIZE = 64
N = 64
DIN = H * P_SIZE
PAIRS = H // 2
EARLY, MIDDLE = 3, 12
HIGHEST = lax.Precision.HIGHEST
F32 = jnp.float32
BF16 = jnp.bfloat16


def from_behind(value, axis, steps):
    count = lax.axis_size(axis)
    leading, last = (max(0, -steps), min(count, count - steps))
    return lax.ppermute(value, axis, [(source, source + steps) for source in range(leading, last)])


def doc_index(lengths, positions):
    starts = jnp.cumsum(lengths) - lengths
    hits = (positions[:, None] >= starts[None, :]).astype(jnp.int32)
    return jnp.sum(hits, axis=1) - 1


def dot(a, b, ca, cb, precision=None):
    return lax.dot_general(
        a, b, (((ca,), (cb,)), ((), ())), precision=precision, preferred_element_type=F32
    )


def core_pair(j, x_ref, dy_ref, steps_ref, skip_ref, dx_ref, rows_ref, xdy_ref, scores, masked, gacc):
    length = x_ref.shape[0]
    where = pl.ds(pl.multiple_of(j * 2 * P_SIZE, 2 * P_SIZE), 2 * P_SIZE)
    x, dy = x_ref[:, where], dy_ref[:, where]
    lane = lax.broadcasted_iota(jnp.int32, (length, 2 * P_SIZE), 1)
    rows = steps_ref[j]
    cols = rows.T
    mixes = []
    total = None
    for h in range(2):
        xh = jnp.where((lane < P_SIZE) == (h == 0), x, jnp.zeros_like(x))
        dw = dot(xh, dy, 1, 1)
        gap = rows[h : h + 1, :] - cols[:, h : h + 1]
        ds = jnp.exp(jnp.minimum(gap, 0.0) + masked[...]) * cols[:, h + 2 : h + 3]
        w = ds * scores[...]
        part = dw * ds
        total = part if total is None else total + part
        rows_ref[j, h + 2 : h + 3, :] = jnp.sum(dw * w, axis=0, keepdims=True)
        mixes.append(dot(w.astype(BF16), dy, 1, 0))
    gacc[...] += total
    mix = jnp.where(lane < P_SIZE, mixes[0], mixes[1])
    xf, dyf = x.astype(F32), dy.astype(F32)
    xm = xf * mix
    high = xm.astype(BF16)
    low = (xm - high.astype(F32)).astype(BF16)
    head = lax.broadcasted_iota(jnp.int32, (8, 2 * P_SIZE), 0)
    pick = lax.broadcasted_iota(jnp.int32, (8, 2 * P_SIZE), 1) // P_SIZE == head
    pick = jnp.where(pick, 1.0, 0.0).astype(BF16)
    rows_ref[j, :2, :] = (dot(pick, high, 1, 1) + dot(pick, low, 1, 1))[:2]
    xdy_ref[j] = jnp.sum(xf * dyf, axis=0, keepdims=True)
    dx_ref[:, where] = (mix + skip_ref[j] * dyf).astype(BF16)


def core_kernel(
    x_ref, dy_ref, steps_ref, docc_ref, docr_ref, skip_ref, parts_ref, decay_ref,
    dx_ref, rows_ref, xdy_ref, dbc_ref, in_ref, adj_ref,
    scores, masked, gacc,
    other, theirs, comb, chain, got, chains, turned, result, lend, landed,
    pair_sems, send_a, recv_a, send_d, recv_d, send_b, recv_b,
):
    length = x_ref.shape[0]
    nc = lax.axis_size("ctx")
    chips = nc // 2
    ctx = lax.axis_index("ctx")
    chip, side = ctx // 2, lax.rem(ctx, 2)
    partner = chip * 2 + 1 - side
    mesh = pl.DeviceIdType.MESH
    rows = parts_ref.shape[2] // 2

    def target(k):
        return lax.rem(chip + k, chips)

    def peer(k):
        return target(k) * 2 + side

    def send(src, dst, sends, recvs, k):
        return pltpu.make_async_remote_copy(
            src_ref=src, dst_ref=dst, send_sem=sends.at[k], recv_sem=recvs.at[k],
            device_id={"ctx": peer(k)}, device_id_type=mesh,
        )

    def swap(src, dst, i):
        return pltpu.make_async_remote_copy(
            src_ref=src, dst_ref=dst, send_sem=pair_sems.at[2 * i], recv_sem=pair_sems.at[2 * i + 1],
            device_id={"ctx": partner}, device_id_type=mesh,
        )

    def both_ways(i):
        half = (i + 1) // 2
        return jnp.where(lax.rem(i, 2) == 1, half, chips - half)

    def pairs(start, stop):
        @pl.loop(start, stop)
        def _(j):
            core_pair(
                j, x_ref, dy_ref, steps_ref, skip_ref, dx_ref, rows_ref, xdy_ref,
                scores, masked, gacc,
            )

    barrier = pltpu.get_barrier_semaphore()
    pl.semaphore_signal(barrier, 1, device_id={"ctx": partner}, device_id_type=mesh)

    @pl.loop(1, chips)
    def _(k):
        pl.semaphore_signal(barrier, 1, device_id={"ctx": peer(k)}, device_id_type=mesh)

    b, c = x_ref[:, DIN : DIN + N], x_ref[:, DIN + N :]
    scores[...] = dot(b, c, 1, 1)
    s = lax.broadcasted_iota(jnp.int32, (length, length), 0)
    t = lax.broadcasted_iota(jnp.int32, (length, length), 1)
    same = (docc_ref[...] == docr_ref[...]) & (t >= s)
    masked[...] = jnp.where(same, 0.0, -1e30)
    gacc[...] = jnp.zeros_like(gacc)
    pairs(0, EARLY)
    pl.semaphore_wait(barrier, chips)

    gives = swap(parts_ref.at[1 - side], other, 0)
    tells = swap(decay_ref, theirs, 1)
    gives.start()
    tells.start()
    gives.wait()
    tells.wait()

    shape = (128, parts_ref.shape[3])
    head = lax.broadcasted_iota(jnp.int32, shape, 1) // P_SIZE + side * (H // 2)
    own = jnp.where(head == lax.broadcasted_iota(jnp.int32, shape, 0), 1.0, 0.0)
    mine, yours = decay_ref[...], theirs[...]
    stacked = jnp.concatenate([jnp.broadcast_to(mine, (8, 128)), jnp.broadcast_to(yours, (8, 128))])
    spread = dot(stacked, own, 1, 0, HIGHEST)
    mine_wide, yours_wide = spread[:8], spread[8:]
    is_forward = lax.broadcasted_iota(jnp.int32, (2 * rows, shape[1]), 0) < rows
    keep_other = is_forward == (side == 0)
    own_gain = jnp.where(keep_other, yours_wide, 1.0)
    other_gain = jnp.where(keep_other, 1.0, mine_wide)
    for i in range(chips):
        comb[i] = (
            own_gain * parts_ref[side, i].astype(F32) + other_gain * other[i].astype(F32)
        ).astype(BF16)
    chain[...] = mine * yours

    def out(k):
        return send(comb.at[target(k)], got.at[chip], send_a, recv_a, k)

    def small(k):
        return send(chain, chains.at[chip], send_d, recv_d, k)

    def back(k):
        return send(turned.at[target(k)], result.at[chip], send_b, recv_b, k)

    @pl.loop(1, chips)
    def _(i):
        small(both_ways(i)).start()
        out(both_ways(i)).start()

    got[chip] = comb[chip]
    chains[chip] = chain[...]
    pairs(EARLY, MIDDLE)

    @pl.loop(1, chips)
    def _(k):
        small(k).wait()
        out(k).wait()

    decay = dot(chains[:, 0, :], own, 1, 0, HIGHEST)
    forward = jnp.zeros((rows, shape[1]), F32)
    for i in range(chips):
        turned[i, :rows] = forward.astype(BF16)
        forward = decay[i : i + 1] * forward + got[i, :rows].astype(F32)
    backward = jnp.zeros((rows, shape[1]), F32)
    for i in reversed(range(chips)):
        turned[i, rows:] = backward.astype(BF16)
        backward = decay[i : i + 1] * backward + got[i, rows:].astype(F32)

    @pl.loop(1, chips)
    def _(i):
        back(both_ways(i)).start()

    result[chip] = turned[chip]
    pairs(MIDDLE, PAIRS)
    g = gacc[...].astype(BF16)
    dbc_ref[:, :N] = dot(g, c, 1, 0)
    dbc_ref[:, N:] = dot(g, b, 0, 0)

    @pl.loop(1, chips)
    def _(k):
        back(k).wait()

    def place(i, half, value):
        lanes = pl.ds(pl.multiple_of(half * shape[1], shape[1]), shape[1])
        in_ref[i * rows : (i + 1) * rows, lanes] = value[:rows]
        adj_ref[i * rows : (i + 1) * rows, lanes] = value[rows:]

    for i in range(chips):
        value = result[i].astype(F32)
        here = jnp.where(keep_other, 1.0, yours_wide) * value
        here = here + jnp.where(keep_other, 0.0, other[i].astype(F32))
        there = jnp.where(keep_other, mine_wide, 1.0) * value
        there = there + jnp.where(keep_other, parts_ref[side, i].astype(F32), 0.0)
        place(i, side, here)
        lend[i] = there.astype(BF16)
    lends = swap(lend, landed, 2)
    lends.start()
    lends.wait()
    for i in range(chips):
        place(i, 1 - side, landed[i].astype(F32))


def core(activated, dy, cum, step, docs, skip_wide, parts, decay):
    length = activated.shape[0]
    chips = parts.shape[1]
    pairs = lambda v: v.reshape(PAIRS, 2, length)
    packed = jnp.concatenate(
        [pairs(cum), pairs(step), jnp.zeros((PAIRS, 4, length), F32)], axis=1
    )
    vmem = pl.BlockSpec(memory_space=pltpu.VMEM)
    dma = pltpu.SemaphoreType.DMA
    half = pltpu.VMEM(parts.shape[1:], BF16)
    line = pltpu.VMEM((1, 128), F32)
    dx, rows, xdy, dbc, incoming, adjoint = pl.pallas_call(
        core_kernel,
        in_specs=[vmem] * 8,
        out_specs=[vmem] * 6,
        out_shape=[
            jax.ShapeDtypeStruct((length, DIN), BF16),
            jax.ShapeDtypeStruct((PAIRS, 4, length), F32),
            jax.ShapeDtypeStruct((PAIRS, 1, 2 * P_SIZE), F32),
            jax.ShapeDtypeStruct((length, 2 * N), F32),
            jax.ShapeDtypeStruct((N, DIN), F32),
            jax.ShapeDtypeStruct((N, DIN), F32),
        ],
        scratch_shapes=[
            *[pltpu.VMEM((length, length), F32)] * 3,
            half, line, half, line, half, pltpu.VMEM((chips, 1, 128), F32),
            half, half, half, half,
            dma((6,)), *[dma((chips,))] * 6,
        ],
        compiler_params=pltpu.CompilerParams(collective_id=1, has_side_effects=True),
        name="core",
    )(
        activated, dy, packed, docs[:, None], docs[None, :],
        skip_wide.reshape(PAIRS, 1, 2 * P_SIZE), parts,
        jnp.pad(decay, (0, 128 - H))[None, :],
    )
    xdx, col = rows[:, :2].reshape(H, length), rows[:, 2:].reshape(H, length)
    return dx, xdx, col, xdy, dbc, incoming, adjoint


def finish_kernel(
    bc_ref, pre_ref, own_ref, rim_ref, taps_ref, keep_ref, tail_ref, weighted_ref, led_ref,
    dx_ref, dbc_ref, in_ref, adj_ref,
    out_ref, edge_ref, grads_ref, lines_ref, met_ref,
    ext, terms, acc,
):
    j = pl.program_id(0)
    length, wide = own_ref.shape
    b, c = bc_ref[:, :N], bc_ref[:, N:]

    def convolve(grad_act):
        grad_act = grad_act.astype(BF16).astype(F32)
        pre = pre_ref[...]
        gate = jax.nn.sigmoid(pre)
        grad_pre = grad_act * (gate * (1.0 + pre * (1.0 - gate)))
        ext[:8] = rim_ref[...]
        ext[8:] = own_ref[...].astype(F32)
        body, edge = None, None
        for k in range(4):
            kept = grad_pre * keep_ref[:, k : k + 1]
            grads_ref[k : k + 1, :] = jnp.sum(
                kept * ext[5 + k : 5 + k + length, :], axis=0, keepdims=True
            )
            terms[k, 8 : 8 + length] = kept * taps_ref[k : k + 1, :]
            here = terms[k, 11 - k : 11 - k + length, :]
            front = terms[k, 8 - k : 16 - k, :]
            body = here if body is None else body + here
            edge = front if edge is None else edge + front
        grads_ref[4:5, :] = jnp.sum(grad_pre, axis=0, keepdims=True)
        grads_ref[5:8, :] = jnp.zeros((3, wide), F32)
        out_ref[...] = body.astype(BF16)
        edge_ref[...] = edge.astype(BF16)

    @pl.when(j == 0)
    def _():
        terms[...] = jnp.zeros_like(terms)
        acc[...] = dbc_ref[...]

    @pl.when(j < PAIRS)
    def _():
        weighted, led = weighted_ref[...], led_ref[...]
        incoming, adjoint = in_ref[...], adj_ref[...]
        met_ref[0] = jnp.sum(incoming * adjoint, axis=0, keepdims=True)
        incoming, adjoint = incoming.astype(BF16), adjoint.astype(BF16)
        outer = dot(c, incoming, 1, 0)
        spread = dot(b, adjoint, 1, 0)
        acc[:, :N] += dot(weighted, adjoint, 1, 1)
        acc[:, N:] += dot(led, incoming, 1, 1)
        head = lax.broadcasted_iota(jnp.int32, (8, wide), 0)
        pick = lax.broadcasted_iota(jnp.int32, (8, wide), 1) // P_SIZE == head
        pick = jnp.where(pick, 1.0, 0.0).astype(BF16)
        values = (led.astype(F32) * outer, spread * weighted.astype(F32))
        for i, value in enumerate(values):
            high = value.astype(BF16)
            low = (value - high.astype(F32)).astype(BF16)
            line = dot(pick, high, 1, 1) + dot(pick, low, 1, 1)
            lines_ref[0, 2 * i : 2 * i + 2, :] = line[:2]
        convolve(dx_ref[...].astype(F32) + spread * tail_ref[...])

    @pl.when(j == PAIRS)
    def _():
        convolve(acc[...])


def finish(
    activated, pre, own_rows, rim_rows, conv_weight, keeps, tail_wide, weighted, led,
    dx, dbc, incoming, adjoint,
):
    length, channels = own_rows.shape
    taps = conv_weight.shape[0]
    wide = 2 * P_SIZE
    every = lambda rows: pl.BlockSpec((rows, wide), lambda j: (0, j))
    inner = lambda rows: pl.BlockSpec((rows, wide), lambda j: (0, jnp.minimum(j, PAIRS - 1)))
    lines = lambda rows, lanes: pl.BlockSpec(
        (1, rows, lanes), lambda j: (jnp.minimum(j, PAIRS - 1), 0, 0)
    )
    fixed = lambda rows, lanes, at: pl.BlockSpec((rows, lanes), lambda j: (0, at))
    return pl.pallas_call(
        finish_kernel,
        grid=(PAIRS + 1,),
        in_specs=[
            fixed(length, wide, PAIRS), every(length), every(length), every(8), every(taps),
            fixed(length, taps, 0), inner(length), inner(length), inner(length),
            inner(length), fixed(length, wide, 0), inner(N), inner(N),
        ],
        out_specs=[every(length), every(8), every(8), lines(4, length), lines(1, wide)],
        out_shape=[
            jax.ShapeDtypeStruct((length, channels), BF16),
            jax.ShapeDtypeStruct((8, channels), BF16),
            jax.ShapeDtypeStruct((8, channels), F32),
            jax.ShapeDtypeStruct((PAIRS, 4, length), F32),
            jax.ShapeDtypeStruct((PAIRS, 1, wide), F32),
        ],
        scratch_shapes=[
            pltpu.VMEM((8 + length, wide), F32),
            pltpu.VMEM((taps, 16 + length, wide), F32),
            pltpu.VMEM((length, wide), F32),
        ],
        name="finish",
    )(
        activated, pre, own_rows, jnp.pad(rim_rows.astype(F32), ((9 - taps, 0), (0, 0))),
        conv_weight, jnp.concatenate(keeps, axis=1).astype(F32), tail_wide, weighted, led,
        dx, dbc, incoming, adjoint,
    )


def total_kernel(
    v_ref, out_ref, got, mid, across, last, spread,
    send_a, recv_a, send_b, recv_b, send_c, recv_c,
):
    nc, nb = lax.axis_size("ctx"), lax.axis_size("bal")
    ctx, bal = lax.axis_index("ctx"), lax.axis_index("bal")

    def to_ctx(k):
        return lax.rem(ctx + k, nc)

    def to_bal(k):
        return lax.rem(bal + k, nb)

    def send(src, dst, sends, recvs, axis, peer, k):
        return pltpu.make_async_remote_copy(
            src_ref=src, dst_ref=dst, send_sem=sends.at[k], recv_sem=recvs.at[k],
            device_id={axis: peer}, device_id_type=pl.DeviceIdType.MESH,
        )

    barrier = pltpu.get_barrier_semaphore()

    @pl.loop(1, nc)
    def _(k):
        pl.semaphore_signal(
            barrier, 1, device_id={"ctx": to_ctx(k)}, device_id_type=pl.DeviceIdType.MESH
        )

    @pl.loop(1, nb)
    def _(k):
        pl.semaphore_signal(
            barrier, 1, device_id={"bal": to_bal(k)}, device_id_type=pl.DeviceIdType.MESH
        )

    pl.semaphore_wait(barrier, nc + nb - 2)

    def first(k):
        return send(v_ref.at[to_ctx(k)], got.at[k], send_a, recv_a, "ctx", to_ctx(k), k)

    def second(k):
        return send(mid, across.at[bal], send_b, recv_b, "bal", to_bal(k), k)

    def third(k):
        return send(last, spread.at[ctx], send_c, recv_c, "ctx", to_ctx(k), k)

    @pl.loop(1, nc)
    def _(k):
        first(k).start()

    got[0] = v_ref[ctx]

    @pl.loop(1, nc)
    def _(k):
        first(k).wait()

    summed = jnp.sum(got[...], axis=0)
    mid[...] = summed
    across[bal] = summed

    @pl.loop(1, nb)
    def _(k):
        second(k).start()

    @pl.loop(1, nb)
    def _(k):
        second(k).wait()

    summed = jnp.sum(across[...], axis=0)
    last[...] = summed
    spread[ctx] = summed

    @pl.loop(1, nc)
    def _(k):
        third(k).start()

    @pl.loop(1, nc)
    def _(k):
        third(k).wait()

    out_ref[...] = spread[...]


def total_sum(vector):
    nc, nb = lax.axis_size("ctx"), lax.axis_size("bal")
    rows = -(-vector.shape[0] // (nc * 128))
    padded = jnp.pad(vector, (0, nc * rows * 128 - vector.shape[0])).reshape(nc, rows, 128)
    dma = pltpu.SemaphoreType.DMA
    summed = pl.pallas_call(
        total_kernel,
        out_shape=jax.ShapeDtypeStruct(padded.shape, F32),
        in_specs=[pl.BlockSpec(memory_space=pltpu.VMEM)],
        out_specs=pl.BlockSpec(memory_space=pltpu.VMEM),
        scratch_shapes=[
            pltpu.VMEM((nc, rows, 128), F32),
            pltpu.VMEM((rows, 128), F32),
            pltpu.VMEM((nb, rows, 128), F32),
            pltpu.VMEM((rows, 128), F32),
            pltpu.VMEM((nc, rows, 128), F32),
            dma((nc,)), dma((nc,)), dma((nb,)), dma((nb,)), dma((nc,)), dma((nc,)),
        ],
        compiler_params=pltpu.CompilerParams(collective_id=0, has_side_effects=True),
        name="total",
    )(padded)
    return summed.reshape(-1)[: vector.shape[0]]


def per_device(xbc, dt_raw, conv_weight, conv_bias, dt_bias, a_log, d_skip, grad_out, doc_lengths):
    taps = conv_weight.shape[0]
    own_rows = xbc[0]
    length = own_rows.shape[0]
    count = lax.axis_size("ctx")
    dy = grad_out[0]
    expand = jnp.asarray(np.kron(np.eye(H), np.ones((1, P_SIZE))), BF16)
    twice = jnp.concatenate([expand, expand])

    def halves(v):
        high = lax.reduce_precision(v, 8, 7)
        return high.astype(BF16), (v - high).astype(BF16)

    widen = lambda v: dot(jnp.concatenate(halves(v)), twice, 0, 0)
    upto = jnp.triu(jnp.ones((length, length), F32))

    offset = lax.axis_index("ctx") * length
    positions = offset + jnp.arange(length + taps - 1, dtype=jnp.int32) - (taps - 1)
    docs_ext = doc_index(doc_lengths[0], positions)
    docs = docs_ext[taps - 1 :]
    prev_doc = docs_ext[taps - 2]
    rim_rows = from_behind(own_rows[length - taps + 1 :], "ctx", 1)
    extended = jnp.concatenate([rim_rows, own_rows], axis=0)
    keeps = [(docs_ext[k : k + length] == docs)[:, None] for k in range(taps)]
    shifted = [
        jnp.where(keeps[k], extended[k : k + length].astype(F32), 0.0) for k in range(taps)
    ]
    pre = conv_bias[None, :]
    for k in range(taps):
        pre = pre + conv_weight[k][None, :] * shifted[k]
    activated = jax.nn.silu(pre).astype(BF16)
    x = activated[:, :DIN].astype(F32)
    b, c = activated[:, DIN : DIN + N], activated[:, DIN + N :]

    raw = dt_raw[0].T.astype(F32) + dt_bias[:, None]
    step = jax.nn.softplus(raw)
    rate = -jnp.exp(a_log)[:, None]
    cum = dot(step * rate, upto, 1, 0, HIGHEST)
    same_last = (docs == docs[-1]).astype(F32)[None, :]
    tail = jnp.exp(cum[:, -1:] - cum) * same_last * step
    lead = jnp.exp(cum) * (docs == prev_doc).astype(F32)[None, :]
    decay = jnp.exp(cum[:, -1]) * (docs[-1] == prev_doc).astype(F32)
    tail_wide = widen(tail)
    weighted = (x * tail_wide).astype(BF16)
    led = (dy.astype(F32) * widen(lead)).astype(BF16)
    local = dot(b, weighted, 0, 0)
    seeded = dot(c, led, 0, 0)

    chips = count // 2
    rows = N // chips
    split = lambda v: v.astype(BF16).reshape(chips, rows, 2, DIN // 2).transpose(2, 0, 1, 3)
    parts = jnp.concatenate([split(local), split(seeded)], axis=2)
    dx, xdx, col, xdy, dbc, incoming, adjoint = core(
        activated, dy, cum, step, docs, jnp.repeat(d_skip, P_SIZE), parts, decay
    )
    own_grad, edge, grad_taps, lines, met = finish(
        activated, pre, own_rows, rim_rows, conv_weight, keeps, tail_wide, weighted, led,
        dx, dbc, incoming, adjoint,
    )
    from_lead = lines[:, :2].reshape(H, length)
    from_tail = lines[:, 2:].reshape(H, length)
    met = jnp.sum(met.reshape(H, P_SIZE), axis=1, keepdims=True)
    grad_last = jnp.sum(from_tail, axis=1, keepdims=True) + met * decay[:, None]
    grad_cum = col - xdx + from_lead - from_tail
    grad_scaled = dot(grad_cum, upto, 1, 1, HIGHEST) + grad_last
    grad_step = (xdx + from_tail) / step + grad_scaled * rate
    grad_alog = jnp.sum(grad_scaled * step, axis=1) * rate[:, 0]
    grad_raw = grad_step * jax.nn.sigmoid(raw)
    grad_raw16 = grad_raw.astype(BF16).T
    grad_dtb = jnp.sum(grad_raw, axis=1)
    grad_skip = jnp.sum(xdy.reshape(H, P_SIZE), axis=1)

    grad_weight, grad_bias = grad_taps[:taps], grad_taps[taps]
    returned = from_behind(edge[: taps - 1], "ctx", -1).astype(F32)
    last = own_grad[length - 8 :].astype(F32) + jnp.pad(returned, ((9 - taps, 0), (0, 0)))
    own_grad = lax.dynamic_update_slice(own_grad, last.astype(BF16), (length - 8, 0))
    mine = (grad_weight, grad_bias, grad_dtb, grad_alog, grad_skip)
    total = total_sum(jnp.concatenate([part.reshape(-1) for part in mine]))
    ends = np.cumsum([part.size for part in mine])[:-1].tolist()
    sums = [part.reshape(like.shape) for part, like in zip(jnp.split(total, ends), mine)]
    return (own_grad[None], grad_raw16[None], *sums)


def solution(mesh):
    in_specs = (
        P("bal", "ctx", None),
        P("bal", "ctx", None),
        P(),
        P(),
        P(),
        P(),
        P(),
        P("bal", "ctx", None),
        P("bal", None),
    )
    out_specs = (P("bal", "ctx", None), P("bal", "ctx", None), P(), P(), P(), P(), P())
    return jax.shard_map(
        per_device, mesh=mesh, in_specs=in_specs, out_specs=out_specs, check_vma=False
    )
```

```python
import jax
import jax.numpy as jnp
import numpy as np
from jax import lax
from jax.experimental import pallas as pl
from jax.experimental.pallas import tpu as pltpu
from jax.sharding import PartitionSpec as P

H = 40
P_SIZE = 64
N = 64
DIN = H * P_SIZE
PAIRS = H // 2
EARLY, MIDDLE = 3, 12
HIGHEST = lax.Precision.HIGHEST
F32 = jnp.float32
BF16 = jnp.bfloat16


def from_behind(value, axis, steps):
    count = lax.axis_size(axis)
    leading, last = (max(0, -steps), min(count, count - steps))
    return lax.ppermute(value, axis, [(source, source + steps) for source in range(leading, last)])


def doc_index(lengths, positions):
    starts = jnp.cumsum(lengths) - lengths
    hits = (positions[:, None] >= starts[None, :]).astype(jnp.int32)
    return jnp.sum(hits, axis=1) - 1


def dot(a, b, ca, cb, precision=None):
    return lax.dot_general(
        a, b, (((ca,), (cb,)), ((), ())), precision=precision, preferred_element_type=F32
    )


def core_pair(j, x_ref, dy_ref, steps_ref, skip_ref, dx_ref, rows_ref, xdy_ref, scores, masked, gacc):
    length = x_ref.shape[0]
    where = pl.ds(pl.multiple_of(j * 2 * P_SIZE, 2 * P_SIZE), 2 * P_SIZE)
    x, dy = x_ref[:, where], dy_ref[:, where]
    lane = lax.broadcasted_iota(jnp.int32, (length, 2 * P_SIZE), 1)
    rows = steps_ref[j]
    cols = rows.T
    mixes = []
    total = None
    for h in range(2):
        xh = jnp.where((lane < P_SIZE) == (h == 0), x, jnp.zeros_like(x))
        dw = dot(xh, dy, 1, 1)
        gap = rows[h : h + 1, :] - cols[:, h : h + 1]
        ds = jnp.exp(jnp.minimum(gap, 0.0) + masked[...]) * cols[:, h + 2 : h + 3]
        w = ds * scores[...]
        part = dw * ds
        total = part if total is None else total + part
        rows_ref[j, h + 2 : h + 3, :] = jnp.sum(dw * w, axis=0, keepdims=True)
        mixes.append(dot(w.astype(BF16), dy, 1, 0))
    gacc[...] += total
    mix = jnp.where(lane < P_SIZE, mixes[0], mixes[1])
    xf, dyf = x.astype(F32), dy.astype(F32)
    xm = xf * mix
    high = xm.astype(BF16)
    low = (xm - high.astype(F32)).astype(BF16)
    head = lax.broadcasted_iota(jnp.int32, (8, 2 * P_SIZE), 0)
    pick = lax.broadcasted_iota(jnp.int32, (8, 2 * P_SIZE), 1) // P_SIZE == head
    pick = jnp.where(pick, 1.0, 0.0).astype(BF16)
    rows_ref[j, :2, :] = (dot(pick, high, 1, 1) + dot(pick, low, 1, 1))[:2]
    xdy_ref[j] = jnp.sum(xf * dyf, axis=0, keepdims=True)
    dx_ref[:, where] = (mix + skip_ref[j] * dyf).astype(BF16)


def core_kernel(
    x_ref, dy_ref, steps_ref, docc_ref, docr_ref, skip_ref, parts_ref, decay_ref,
    dx_ref, rows_ref, xdy_ref, dbc_ref, in_ref, adj_ref,
    scores, masked, gacc,
    other, theirs, comb, chain, got, chains, turned, result, lend, landed,
    pair_sems, send_a, recv_a, send_d, recv_d, send_b, recv_b,
):
    length = x_ref.shape[0]
    nc = lax.axis_size("ctx")
    chips = nc // 2
    ctx = lax.axis_index("ctx")
    chip, side = ctx // 2, lax.rem(ctx, 2)
    partner = chip * 2 + 1 - side
    mesh = pl.DeviceIdType.MESH
    rows = parts_ref.shape[2] // 2

    def target(k):
        return lax.rem(chip + k, chips)

    def peer(k):
        return target(k) * 2 + side

    def send(src, dst, sends, recvs, k):
        return pltpu.make_async_remote_copy(
            src_ref=src, dst_ref=dst, send_sem=sends.at[k], recv_sem=recvs.at[k],
            device_id={"ctx": peer(k)}, device_id_type=mesh,
        )

    def swap(src, dst, i):
        return pltpu.make_async_remote_copy(
            src_ref=src, dst_ref=dst, send_sem=pair_sems.at[2 * i], recv_sem=pair_sems.at[2 * i + 1],
            device_id={"ctx": partner}, device_id_type=mesh,
        )

    def both_ways(i):
        half = (i + 1) // 2
        return jnp.where(lax.rem(i, 2) == 1, half, chips - half)

    def pairs(start, stop):
        @pl.loop(start, stop)
        def _(j):
            core_pair(
                j, x_ref, dy_ref, steps_ref, skip_ref, dx_ref, rows_ref, xdy_ref,
                scores, masked, gacc,
            )

    barrier = pltpu.get_barrier_semaphore()
    pl.semaphore_signal(barrier, 1, device_id={"ctx": partner}, device_id_type=mesh)

    @pl.loop(1, chips)
    def _(k):
        pl.semaphore_signal(barrier, 1, device_id={"ctx": peer(k)}, device_id_type=mesh)

    b, c = x_ref[:, DIN : DIN + N], x_ref[:, DIN + N :]
    scores[...] = dot(b, c, 1, 1)
    s = lax.broadcasted_iota(jnp.int32, (length, length), 0)
    t = lax.broadcasted_iota(jnp.int32, (length, length), 1)
    same = (docc_ref[...] == docr_ref[...]) & (t >= s)
    masked[...] = jnp.where(same, 0.0, -1e30)
    gacc[...] = jnp.zeros_like(gacc)
    pairs(0, EARLY)
    pl.semaphore_wait(barrier, chips)

    gives = swap(parts_ref.at[1 - side], other, 0)
    tells = swap(decay_ref, theirs, 1)
    gives.start()
    tells.start()
    gives.wait()
    tells.wait()

    shape = (128, parts_ref.shape[3])
    head = lax.broadcasted_iota(jnp.int32, shape, 1) // P_SIZE + side * (H // 2)
    own = jnp.where(head == lax.broadcasted_iota(jnp.int32, shape, 0), 1.0, 0.0)
    mine, yours = decay_ref[...], theirs[...]
    stacked = jnp.concatenate([jnp.broadcast_to(mine, (8, 128)), jnp.broadcast_to(yours, (8, 128))])
    spread = dot(stacked, own, 1, 0, HIGHEST)
    mine_wide, yours_wide = spread[:8], spread[8:]
    is_forward = lax.broadcasted_iota(jnp.int32, (2 * rows, shape[1]), 0) < rows
    keep_other = is_forward == (side == 0)
    own_gain = jnp.where(keep_other, yours_wide, 1.0)
    other_gain = jnp.where(keep_other, 1.0, mine_wide)
    for i in range(chips):
        comb[i] = (
            own_gain * parts_ref[side, i].astype(F32) + other_gain * other[i].astype(F32)
        ).astype(BF16)
    chain[...] = mine * yours

    def out(k):
        return send(comb.at[target(k)], got.at[chip], send_a, recv_a, k)

    def small(k):
        return send(chain, chains.at[chip], send_d, recv_d, k)

    def back(k):
        return send(turned.at[target(k)], result.at[chip], send_b, recv_b, k)

    @pl.loop(1, chips)
    def _(i):
        small(both_ways(i)).start()
        out(both_ways(i)).start()

    got[chip] = comb[chip]
    chains[chip] = chain[...]
    pairs(EARLY, MIDDLE)

    @pl.loop(1, chips)
    def _(k):
        small(k).wait()
        out(k).wait()

    decay = dot(chains[:, 0, :], own, 1, 0, HIGHEST)
    forward = jnp.zeros((rows, shape[1]), F32)
    for i in range(chips):
        turned[i, :rows] = forward.astype(BF16)
        forward = decay[i : i + 1] * forward + got[i, :rows].astype(F32)
    backward = jnp.zeros((rows, shape[1]), F32)
    for i in reversed(range(chips)):
        turned[i, rows:] = backward.astype(BF16)
        backward = decay[i : i + 1] * backward + got[i, rows:].astype(F32)

    @pl.loop(1, chips)
    def _(i):
        back(both_ways(i)).start()

    result[chip] = turned[chip]
    pairs(MIDDLE, PAIRS)
    g = gacc[...].astype(BF16)
    dbc_ref[:, :N] = dot(g, c, 1, 0)
    dbc_ref[:, N:] = dot(g, b, 0, 0)

    @pl.loop(1, chips)
    def _(k):
        back(k).wait()

    def place(i, half, value):
        lanes = pl.ds(pl.multiple_of(half * shape[1], shape[1]), shape[1])
        in_ref[i * rows : (i + 1) * rows, lanes] = value[:rows]
        adj_ref[i * rows : (i + 1) * rows, lanes] = value[rows:]

    for i in range(chips):
        value = result[i].astype(F32)
        here = jnp.where(keep_other, 1.0, yours_wide) * value
        here = here + jnp.where(keep_other, 0.0, other[i].astype(F32))
        there = jnp.where(keep_other, mine_wide, 1.0) * value
        there = there + jnp.where(keep_other, parts_ref[side, i].astype(F32), 0.0)
        place(i, side, here)
        lend[i] = there.astype(BF16)
    lends = swap(lend, landed, 2)
    lends.start()
    lends.wait()
    for i in range(chips):
        place(i, 1 - side, landed[i].astype(F32))


def core(activated, dy, cum, step, docs, skip_wide, parts, decay):
    length = activated.shape[0]
    chips = parts.shape[1]
    pairs = lambda v: v.reshape(PAIRS, 2, length)
    packed = jnp.concatenate(
        [pairs(cum), pairs(step), jnp.zeros((PAIRS, 4, length), F32)], axis=1
    )
    vmem = pl.BlockSpec(memory_space=pltpu.VMEM)
    dma = pltpu.SemaphoreType.DMA
    half = pltpu.VMEM(parts.shape[1:], BF16)
    line = pltpu.VMEM((1, 128), F32)
    dx, rows, xdy, dbc, incoming, adjoint = pl.pallas_call(
        core_kernel,
        in_specs=[vmem] * 8,
        out_specs=[vmem] * 6,
        out_shape=[
            jax.ShapeDtypeStruct((length, DIN), BF16),
            jax.ShapeDtypeStruct((PAIRS, 4, length), F32),
            jax.ShapeDtypeStruct((PAIRS, 1, 2 * P_SIZE), F32),
            jax.ShapeDtypeStruct((length, 2 * N), F32),
            jax.ShapeDtypeStruct((N, DIN), F32),
            jax.ShapeDtypeStruct((N, DIN), F32),
        ],
        scratch_shapes=[
            *[pltpu.VMEM((length, length), F32)] * 3,
            half, line, half, line, half, pltpu.VMEM((chips, 1, 128), F32),
            half, half, half, half,
            dma((6,)), *[dma((chips,))] * 6,
        ],
        compiler_params=pltpu.CompilerParams(collective_id=1, has_side_effects=True),
        name="core",
    )(
        activated, dy, packed, docs[:, None], docs[None, :],
        skip_wide.reshape(PAIRS, 1, 2 * P_SIZE), parts,
        jnp.pad(decay, (0, 128 - H))[None, :],
    )
    xdx, col = rows[:, :2].reshape(H, length), rows[:, 2:].reshape(H, length)
    return dx, xdx, col, xdy, dbc, incoming, adjoint


def finish_kernel(
    bc_ref, pre_ref, own_ref, rim_ref, taps_ref, keep_ref, tail_ref, weighted_ref, led_ref,
    dx_ref, dbc_ref, in_ref, adj_ref,
    out_ref, edge_ref, grads_ref, lines_ref, met_ref,
    ext, terms, acc,
):
    j = pl.program_id(0)
    length, wide = own_ref.shape
    b, c = bc_ref[:, :N], bc_ref[:, N:]

    def convolve(grad_act):
        grad_act = grad_act.astype(BF16).astype(F32)
        pre = pre_ref[...]
        gate = jax.nn.sigmoid(pre)
        grad_pre = grad_act * (gate * (1.0 + pre * (1.0 - gate)))
        ext[:8] = rim_ref[...]
        ext[8:] = own_ref[...].astype(F32)
        body, edge = None, None
        for k in range(4):
            kept = grad_pre * keep_ref[:, k : k + 1]
            grads_ref[k : k + 1, :] = jnp.sum(
                kept * ext[5 + k : 5 + k + length, :], axis=0, keepdims=True
            )
            terms[k, 8 : 8 + length] = kept * taps_ref[k : k + 1, :]
            here = terms[k, 11 - k : 11 - k + length, :]
            front = terms[k, 8 - k : 16 - k, :]
            body = here if body is None else body + here
            edge = front if edge is None else edge + front
        grads_ref[4:5, :] = jnp.sum(grad_pre, axis=0, keepdims=True)
        grads_ref[5:8, :] = jnp.zeros((3, wide), F32)
        out_ref[...] = body.astype(BF16)
        edge_ref[...] = edge.astype(BF16)

    @pl.when(j == 0)
    def _():
        terms[...] = jnp.zeros_like(terms)
        acc[...] = dbc_ref[...]

    @pl.when(j < PAIRS)
    def _():
        weighted, led = weighted_ref[...], led_ref[...]
        incoming, adjoint = in_ref[...], adj_ref[...]
        met_ref[0] = jnp.sum(incoming * adjoint, axis=0, keepdims=True)
        incoming, adjoint = incoming.astype(BF16), adjoint.astype(BF16)
        outer = dot(c, incoming, 1, 0)
        spread = dot(b, adjoint, 1, 0)
        acc[:, :N] += dot(weighted, adjoint, 1, 1)
        acc[:, N:] += dot(led, incoming, 1, 1)
        head = lax.broadcasted_iota(jnp.int32, (8, wide), 0)
        pick = lax.broadcasted_iota(jnp.int32, (8, wide), 1) // P_SIZE == head
        pick = jnp.where(pick, 1.0, 0.0).astype(BF16)
        values = (led.astype(F32) * outer, spread * weighted.astype(F32))
        for i, value in enumerate(values):
            high = value.astype(BF16)
            low = (value - high.astype(F32)).astype(BF16)
            line = dot(pick, high, 1, 1) + dot(pick, low, 1, 1)
            lines_ref[0, 2 * i : 2 * i + 2, :] = line[:2]
        convolve(dx_ref[...].astype(F32) + spread * tail_ref[...])

    @pl.when(j == PAIRS)
    def _():
        convolve(acc[...])


def finish(
    activated, pre, own_rows, rim_rows, conv_weight, keeps, tail_wide, weighted, led,
    dx, dbc, incoming, adjoint,
):
    length, channels = own_rows.shape
    taps = conv_weight.shape[0]
    wide = 2 * P_SIZE
    every = lambda rows: pl.BlockSpec((rows, wide), lambda j: (0, j))
    inner = lambda rows: pl.BlockSpec((rows, wide), lambda j: (0, jnp.minimum(j, PAIRS - 1)))
    lines = lambda rows, lanes: pl.BlockSpec(
        (1, rows, lanes), lambda j: (jnp.minimum(j, PAIRS - 1), 0, 0)
    )
    fixed = lambda rows, lanes, at: pl.BlockSpec((rows, lanes), lambda j: (0, at))
    return pl.pallas_call(
        finish_kernel,
        grid=(PAIRS + 1,),
        in_specs=[
            fixed(length, wide, PAIRS), every(length), every(length), every(8), every(taps),
            fixed(length, taps, 0), inner(length), inner(length), inner(length),
            inner(length), fixed(length, wide, 0), inner(N), inner(N),
        ],
        out_specs=[every(length), every(8), every(8), lines(4, length), lines(1, wide)],
        out_shape=[
            jax.ShapeDtypeStruct((length, channels), BF16),
            jax.ShapeDtypeStruct((8, channels), BF16),
            jax.ShapeDtypeStruct((8, channels), F32),
            jax.ShapeDtypeStruct((PAIRS, 4, length), F32),
            jax.ShapeDtypeStruct((PAIRS, 1, wide), F32),
        ],
        scratch_shapes=[
            pltpu.VMEM((8 + length, wide), F32),
            pltpu.VMEM((taps, 16 + length, wide), F32),
            pltpu.VMEM((length, wide), F32),
        ],
        name="finish",
    )(
        activated, pre, own_rows, jnp.pad(rim_rows.astype(F32), ((9 - taps, 0), (0, 0))),
        conv_weight, jnp.concatenate(keeps, axis=1).astype(F32), tail_wide, weighted, led,
        dx, dbc, incoming, adjoint,
    )


def total_kernel(
    wide_ref, small_ref, wide_out, small_out, v_ref, got, mid, across, last, spread,
    send_a, recv_a, send_b, recv_b, send_c, recv_c,
):
    nc, nb = lax.axis_size("ctx"), lax.axis_size("bal")
    ctx, bal = lax.axis_index("ctx"), lax.axis_index("bal")

    def to_ctx(k):
        return lax.rem(ctx + k, nc)

    def to_bal(k):
        return lax.rem(bal + k, nb)

    def send(src, dst, sends, recvs, axis, peer, k):
        return pltpu.make_async_remote_copy(
            src_ref=src, dst_ref=dst, send_sem=sends.at[k], recv_sem=recvs.at[k],
            device_id={axis: peer}, device_id_type=pl.DeviceIdType.MESH,
        )

    blocks = wide_ref.shape[1] // 128
    for i in range(blocks):
        v_ref[i] = wide_ref[:, i * 128 : (i + 1) * 128]
    v_ref[blocks] = small_ref[...]
    v_ref[blocks + 1 :] = jnp.zeros((nc - blocks - 1, *small_ref.shape), F32)

    barrier = pltpu.get_barrier_semaphore()

    @pl.loop(1, nc)
    def _(k):
        pl.semaphore_signal(
            barrier, 1, device_id={"ctx": to_ctx(k)}, device_id_type=pl.DeviceIdType.MESH
        )

    @pl.loop(1, nb)
    def _(k):
        pl.semaphore_signal(
            barrier, 1, device_id={"bal": to_bal(k)}, device_id_type=pl.DeviceIdType.MESH
        )

    pl.semaphore_wait(barrier, nc + nb - 2)

    def first(k):
        return send(v_ref.at[to_ctx(k)], got.at[k], send_a, recv_a, "ctx", to_ctx(k), k)

    def second(k):
        return send(mid, across.at[bal], send_b, recv_b, "bal", to_bal(k), k)

    def third(k):
        return send(last, spread.at[ctx], send_c, recv_c, "ctx", to_ctx(k), k)

    @pl.loop(1, nc)
    def _(k):
        first(k).start()

    got[0] = v_ref[ctx]

    @pl.loop(1, nc)
    def _(k):
        first(k).wait()

    summed = jnp.sum(got[...], axis=0)
    mid[...] = summed
    across[bal] = summed

    @pl.loop(1, nb)
    def _(k):
        second(k).start()

    @pl.loop(1, nb)
    def _(k):
        second(k).wait()

    summed = jnp.sum(across[...], axis=0)
    last[...] = summed
    spread[ctx] = summed

    @pl.loop(1, nc)
    def _(k):
        third(k).start()

    @pl.loop(1, nc)
    def _(k):
        third(k).wait()

    for i in range(blocks):
        wide_out[:, i * 128 : (i + 1) * 128] = spread[i]
    small_out[...] = spread[blocks]


def total_sum(wide, small):
    nc, nb = lax.axis_size("ctx"), lax.axis_size("bal")
    piece = small.shape
    vmem = pl.BlockSpec(memory_space=pltpu.VMEM)
    dma = pltpu.SemaphoreType.DMA
    return pl.pallas_call(
        total_kernel,
        out_shape=[jax.ShapeDtypeStruct(wide.shape, F32), jax.ShapeDtypeStruct(piece, F32)],
        in_specs=[vmem] * 2,
        out_specs=[vmem] * 2,
        scratch_shapes=[
            pltpu.VMEM((nc, *piece), F32),
            pltpu.VMEM((nc, *piece), F32),
            pltpu.VMEM(piece, F32),
            pltpu.VMEM((nb, *piece), F32),
            pltpu.VMEM(piece, F32),
            pltpu.VMEM((nc, *piece), F32),
            dma((nc,)), dma((nc,)), dma((nb,)), dma((nb,)), dma((nc,)), dma((nc,)),
        ],
        compiler_params=pltpu.CompilerParams(collective_id=0, has_side_effects=True),
        name="total",
    )(wide, small)


def per_device(xbc, dt_raw, conv_weight, conv_bias, dt_bias, a_log, d_skip, grad_out, doc_lengths):
    taps = conv_weight.shape[0]
    own_rows = xbc[0]
    length = own_rows.shape[0]
    count = lax.axis_size("ctx")
    dy = grad_out[0]
    expand = jnp.asarray(np.kron(np.eye(H), np.ones((1, P_SIZE))), BF16)
    twice = jnp.concatenate([expand, expand])

    def halves(v):
        high = lax.reduce_precision(v, 8, 7)
        return high.astype(BF16), (v - high).astype(BF16)

    widen = lambda v: dot(jnp.concatenate(halves(v)), twice, 0, 0)
    upto = jnp.triu(jnp.ones((length, length), F32))

    offset = lax.axis_index("ctx") * length
    positions = offset + jnp.arange(length + taps - 1, dtype=jnp.int32) - (taps - 1)
    docs_ext = doc_index(doc_lengths[0], positions)
    docs = docs_ext[taps - 1 :]
    prev_doc = docs_ext[taps - 2]
    rim_rows = from_behind(own_rows[length - taps + 1 :], "ctx", 1)
    extended = jnp.concatenate([rim_rows, own_rows], axis=0)
    keeps = [(docs_ext[k : k + length] == docs)[:, None] for k in range(taps)]
    shifted = [
        jnp.where(keeps[k], extended[k : k + length].astype(F32), 0.0) for k in range(taps)
    ]
    pre = conv_bias[None, :]
    for k in range(taps):
        pre = pre + conv_weight[k][None, :] * shifted[k]
    activated = jax.nn.silu(pre).astype(BF16)
    x = activated[:, :DIN].astype(F32)
    b, c = activated[:, DIN : DIN + N], activated[:, DIN + N :]

    raw = dt_raw[0].T.astype(F32) + dt_bias[:, None]
    step = jax.nn.softplus(raw)
    rate = -jnp.exp(a_log)[:, None]
    cum = dot(step * rate, upto, 1, 0, HIGHEST)
    same_last = (docs == docs[-1]).astype(F32)[None, :]
    tail = jnp.exp(cum[:, -1:] - cum) * same_last * step
    lead = jnp.exp(cum) * (docs == prev_doc).astype(F32)[None, :]
    decay = jnp.exp(cum[:, -1]) * (docs[-1] == prev_doc).astype(F32)
    tail_wide = widen(tail)
    weighted = (x * tail_wide).astype(BF16)
    led = (dy.astype(F32) * widen(lead)).astype(BF16)
    local = dot(b, weighted, 0, 0)
    seeded = dot(c, led, 0, 0)

    chips = count // 2
    rows = N // chips
    split = lambda v: v.astype(BF16).reshape(chips, rows, 2, DIN // 2).transpose(2, 0, 1, 3)
    parts = jnp.concatenate([split(local), split(seeded)], axis=2)
    dx, xdx, col, xdy, dbc, incoming, adjoint = core(
        activated, dy, cum, step, docs, jnp.repeat(d_skip, P_SIZE), parts, decay
    )
    own_grad, edge, grad_taps, lines, met = finish(
        activated, pre, own_rows, rim_rows, conv_weight, keeps, tail_wide, weighted, led,
        dx, dbc, incoming, adjoint,
    )
    from_lead = lines[:, :2].reshape(H, length)
    from_tail = lines[:, 2:].reshape(H, length)
    met = jnp.sum(met.reshape(H, P_SIZE), axis=1, keepdims=True)
    grad_last = jnp.sum(from_tail, axis=1, keepdims=True) + met * decay[:, None]
    grad_cum = col - xdx + from_lead - from_tail
    grad_scaled = dot(grad_cum, upto, 1, 1, HIGHEST) + grad_last
    grad_step = (xdx + from_tail) / step + grad_scaled * rate
    grad_alog = jnp.sum(grad_scaled * step, axis=1) * rate[:, 0]
    grad_raw = grad_step * jax.nn.sigmoid(raw)
    grad_raw16 = grad_raw.astype(BF16).T
    grad_dtb = jnp.sum(grad_raw, axis=1)
    grad_skip = jnp.sum(xdy.reshape(H, P_SIZE), axis=1)

    returned = from_behind(edge[: taps - 1], "ctx", -1).astype(F32)
    last = own_grad[length - 8 :].astype(F32) + jnp.pad(returned, ((9 - taps, 0), (0, 0)))
    own_grad = lax.dynamic_update_slice(own_grad, last.astype(BF16), (length - 8, 0))
    small = jnp.pad(jnp.stack([grad_dtb, grad_alog, grad_skip]), ((0, 5), (0, 128 - H)))
    wide, small = total_sum(grad_taps, small)
    sums = (wide[:taps], wide[taps], small[0, :H], small[1, :H], small[2, :H])
    return (own_grad[None], grad_raw16[None], *sums)


def solution(mesh):
    in_specs = (
        P("bal", "ctx", None),
        P("bal", "ctx", None),
        P(),
        P(),
        P(),
        P(),
        P(),
        P("bal", "ctx", None),
        P("bal", None),
    )
    out_specs = (P("bal", "ctx", None), P("bal", "ctx", None), P(), P(), P(), P(), P())
    return jax.shard_map(
        per_device, mesh=mesh, in_specs=in_specs, out_specs=out_specs, check_vma=False
    )
```
